128 devices in a mesh: depth: 16 (over x_hi, y, core), seq: 8 (over z, x_lo).
Axes of the slice: x: 4 (x_hi: 2, x_lo: 2; x = x_hi * 2 + x_lo), y: 4, z: 4, core: 2. Of those that a mesh axis runs over, the one named last changes fastest.
Arguments:
- interfaces: bfloat16 [16, 1, 2048, 1024], P('depth', None, 'seq'), may hold values from -6 to 6
- doc_ids: int32 [1, 2048], replicated, may hold values from 0 to 3, never falling along the last dimension, each value on 1 to 1024 neighbouring positions
- w_attn: bfloat16 [16, 1, 4, 1024, 1024], P('depth'), may hold values from -0.1875 to 0.1875
- w_up: bfloat16 [16, 1, 1024, 4096], P('depth'), may hold values from -0.1875 to 0.1875
- w_down: bfloat16 [16, 1, 4096, 1024], P('depth'), may hold values from -0.09375 to 0.09375
- norm_gains: float32 [16, 1, 2, 1024], P('depth'), may hold values from 0.25 to 1.75
- coarse_gain: float32 [16, 1024], P('depth'), may hold values from 0 to 1
Outputs:
- relaxed: bfloat16 [16, 1, 2048, 1024], P('depth', None, 'seq')
The draws below stay inside these ranges and needn't reach their ends.
Inputs may be any that keep to these rules, and one draw needn't show every extreme that they name: doc_ids never fall along a sequence and number the documents packed into it.
All inputs are finite; a program needn't handle non-finite values.
Results may differ from the reference program's by a relative error of at most 0.025.
Values may be sent and summed in bfloat16 or wider, within the bound.
A program may use at most 192 MiB of HBM per device.

```python
import math
import jax
import jax.numpy as jnp
import numpy as np
from jax import lax

D = 1024
FF = 4096
HEADS = 16
SEC_LAYERS = 1
LEN = 2048
SEQS = 1
LAYER_SPANS = 16


def draw_coarse_gain(key, part):
    first_key = jax.random.fold_in(key, 11)
    second_key = jax.random.fold_in(key, 12)
    lookup_slice_final = jax.random.fold_in(key, 13)
    decay_rate = jnp.exp(jax.random.uniform(first_key, (D,), jnp.float32, math.log(0.3 / LAYER_SPANS), math.log(3.0)))
    dispersion = jax.random.uniform(second_key, (LAYER_SPANS, D), jnp.float32, 0.5, 2.0)
    packet_clusters = jax.random.bernoulli(lookup_slice_final, 2.0 / LAYER_SPANS, (LAYER_SPANS, 1))
    multiplier_coefficient = jnp.where(packet_clusters, 0.6, 1.0).astype(jnp.float32)
    return (jnp.exp(-decay_rate[None, :] * dispersion) * multiplier_coefficient).astype(jnp.float32)


def shard_levels(key, extent, cuts, low, largest):
    def one(dim, blocks):
        draws = jax.random.uniform(jax.random.fold_in(jax.random.fold_in(key, 6), dim), (blocks,), jnp.float32, low / len(cuts), largest / len(cuts))
        return jnp.repeat(jnp.exp(draws), extent[dim] // blocks).reshape((-1,) + (1,) * (len(extent) - dim - 1))

    level = one(*cuts[0])
    for cut in cuts[1:]:
        level = level * one(*cut)
    return level


def split_up(amount, total, limit, skew):
    loads = [(1 << 20) // math.isqrt(rank ** skew) + 1 for rank in range(2, amount + 1)]
    spare, given = total - limit - (amount - 1), [1] * (amount - 1)
    while spare > 0:
        movable = [i for i in range(amount - 1) if given[i] < limit]
        whole, remaining = sum([loads[i] for i in movable]), spare
        for i in movable:
            extra = min(limit - given[i], max(1, remaining * loads[i] // whole), spare)
            given[i] = given[i] + extra
            spare = spare - extra
    return np.array([limit] + given)


def uneven(rng, amount, total, bound, lean):
    if amount == 2:
        one = jax.random.randint(rng, (), max(1, total - bound), min(bound, total - 1) + 1)
        return jnp.stack([one, total - one])
    sizes = jnp.asarray(split_up(amount, total, bound, lean), jnp.int32)
    twos = (amount - 1) // 2
    giver, receiver = sizes[1:1 + 2 * twos:2], sizes[2:2 + 2 * twos:2]
    margin = jnp.minimum(giver - 1, bound - receiver)
    shifted = jax.random.randint(jax.random.fold_in(rng, 1), (twos,), 0, 1 << 20) % (margin + 1)
    sizes = sizes.at[1:1 + 2 * twos:2].set(giver - shifted).at[2:2 + 2 * twos:2].set(receiver + shifted)
    return sizes[jax.random.permutation(jax.random.fold_in(rng, 2), amount)]


def bell_draw(rng, extent, spread, bound, pieces=(), kind=jnp.bfloat16):
    level = shard_levels(rng, extent, pieces, -0.22, 0.18) if pieces else 1.0
    values = jax.random.normal(rng, extent, jnp.float32) * spread * level
    return jnp.minimum(jnp.maximum(values, -bound), bound).astype(kind)


def setup_inputs(seed: int = 0) -> dict:
    arg_keys = jax.random.split(jax.random.key(seed), 8)
    return {
        "interfaces": bell_draw(arg_keys[0], (LAYER_SPANS, SEQS, LEN, D), 1.0, 6.0, ((0, 16), (2, 8))),
        "doc_ids": jax.vmap(lambda own: jnp.searchsorted(jnp.cumsum(uneven(own, 4, LEN, LEN // 2, 1)), jnp.arange(LEN), side="right"))(jax.random.split(arg_keys[1], SEQS)).reshape((SEQS, LEN)).astype(jnp.int32),
        "w_attn": bell_draw(arg_keys[2], (LAYER_SPANS, SEC_LAYERS, 4, D, D), D ** -0.5, 0.1875, ((0, 16),)),
        "w_up": bell_draw(arg_keys[3], (LAYER_SPANS, SEC_LAYERS, D, FF), D ** -0.5, 0.1875, ((0, 16),)),
        "w_down": bell_draw(arg_keys[4], (LAYER_SPANS, SEC_LAYERS, FF, D), FF ** -0.5, 0.09375, ((0, 16),)),
        "norm_gains": jnp.clip(1.0 + 0.15 * jax.random.normal(arg_keys[5], (LAYER_SPANS, SEC_LAYERS, 2, D), jnp.float32), 0.25, 1.75),
        "coarse_gain": draw_coarse_gain(jax.random.fold_in(arg_keys[7], 71), 0),
    }


def rms_norm(value_tensor, gain):
    return value_tensor * lax.rsqrt(lax.optimization_barrier(jnp.mean(value_tensor * value_tensor, axis=-1, keepdims=True)) + 1e-05) * gain

def one_layer(states, attn_w, up_w, lowering_matrix, gain_pair, doc_ids):
    batch, rows, width = states.shape
    head_dim = width // HEADS
    normed = rms_norm(states.astype(jnp.float32), gain_pair[0]).astype(jnp.bfloat16)
    flat = normed.reshape(-1, width)
    queries = jnp.dot(flat, attn_w[0], preferred_element_type=jnp.float32).astype(jnp.bfloat16).reshape(batch, rows, HEADS, head_dim)
    keys_all = jnp.dot(flat, attn_w[1], preferred_element_type=jnp.float32).astype(jnp.bfloat16).reshape(batch, rows, HEADS, head_dim)
    values_all = jnp.dot(flat, attn_w[2], preferred_element_type=jnp.float32).astype(jnp.bfloat16).reshape(batch, rows, HEADS, head_dim)
    scores = jnp.einsum('sqhd,skhd->shqk', queries.astype(jnp.float32), keys_all.astype(jnp.float32)) * head_dim ** (-0.5)
    position = jnp.arange(rows)
    causal = position[None, :] <= position[:, None]
    same_doc = doc_ids[:, :, None] == doc_ids[:, None, :]
    allowed = (causal[None] & same_doc)[:, None]
    weights = jnp.where(allowed, jnp.exp(scores), jnp.zeros_like(scores))
    denominator = lax.optimization_barrier(jnp.sum(weights, axis=-1))
    numerator = jnp.einsum('shqk,skhd->shqd', weights.astype(jnp.bfloat16).astype(jnp.float32), values_all.astype(jnp.float32))
    attended = (numerator / denominator[..., None]).transpose(0, 2, 1, 3).reshape(batch * rows, width).astype(jnp.bfloat16)
    mixed = states.astype(jnp.float32) + jnp.dot(attended, attn_w[3], preferred_element_type=jnp.float32).reshape(batch, rows, width)
    second = rms_norm(mixed, gain_pair[1]).astype(jnp.bfloat16).reshape(-1, width)
    expanded = jax.nn.gelu(jnp.dot(second, up_w, preferred_element_type=jnp.float32)).astype(jnp.bfloat16)
    result = mixed + jnp.dot(expanded, lowering_matrix, preferred_element_type=jnp.float32).reshape(batch, rows, width)
    return result.astype(jnp.bfloat16)

def reference(interfaces, doc_ids, w_attn, w_up, w_down, norm_gains, coarse_gain):

    def section(operands):
        states, attn_stack, up_stack, down_stack, gain_stack = operands
        for layer_idx in range(SEC_LAYERS):
            states = one_layer(states, attn_stack[layer_idx], up_stack[layer_idx], down_stack[layer_idx], gain_stack[layer_idx], doc_ids)
        return states

    def relax(starting):
        return lax.map(section, (starting, w_attn, w_up, w_down, norm_gains))
    fine = relax(interfaces)
    following = jnp.concatenate([interfaces[1:], jnp.zeros_like(interfaces[:1])], axis=0)
    mismatch = fine.astype(jnp.float32) - following.astype(jnp.float32)

    def advance(correction, inputs_now):
        multiplier_coefficient, gap = inputs_now
        return (multiplier_coefficient[None, None, :] * correction + gap, correction)
    start_zero = jnp.zeros(interfaces.shape[1:], jnp.float32)
    unused, correction = lax.scan(advance, start_zero, (coarse_gain, mismatch))
    corrected = (interfaces.astype(jnp.float32) + correction).astype(jnp.bfloat16)
    return relax(corrected)
```

```python
import functools

import jax
import jax.numpy as jnp
from jax import lax
from jax.experimental import pallas as pl
from jax.experimental.pallas import tpu as pltpu
from jax.sharding import Mesh
from jax.sharding import PartitionSpec as P

D = 1024
FF = 4096
ROWS = 256
LANES = 128
HEAD = 64
GROUPS = 8
SPAN = 5
SEQ = ("seq_0", "seq_1")
DEPTH = ("depth_0", "depth_1", "depth_2")
MESH = pl.DeviceIdType.MESH
SEQ_STEPS = [(a, b) for a in range(4) for b in range(2) if (a, b) != (0, 0)]
DEPTH_STEPS = [(a, b) for a in range(2) for b in range(4) if (a, b) != (0, 0)]
K, Q, V, A = 0, 1, 2, 3
NT = (((1,), (1,)), ((), ()))


def dot(a, b):
    return jnp.dot(a, b, preferred_element_type=jnp.float32)


def rms(value, gain):
    return value * lax.rsqrt(jnp.mean(value * value, axis=-1, keepdims=True) + 1e-05) * gain


def kernel(
    x_ref, doc_ref, gain_ref, coarse_ref, wa_hbm, wu_hbm, wd_hbm, o_ref,
    wa, wu, wd, xs, nb, stage, stage_v, kr, qr, vr, mask, prob, stage_a, ar, mixed, second, acc,
    gains, fine, half_in, comp, depth_a, depth_u, depth_r, given, corrected,
    w_sem, send_sem, recv_sem, dsend_sem, drecv_sem, csend_sem, crecv_sem,
):
    h, y, core = (lax.axis_index(a) for a in DEPTH)
    z, c = (lax.axis_index(a) for a in SEQ)
    me = 2 * z + c
    chip = 4 * h + y

    def seq_peer(step):
        pz, pc = lax.rem(z + step[0], 4), lax.rem(c + step[1], 2)
        return (h, y, core, pz, pc), 2 * pz + pc

    def seq_from(step):
        pz, pc = lax.rem(z + 4 - step[0], 4), lax.rem(c + step[1], 2)
        return 2 * pz + pc

    def depth_peer(step):
        ph, py = lax.rem(h + step[0], 2), lax.rem(y + step[1], 4)
        return (ph, py, core, z, c), 4 * ph + py

    partner = (h, y, 1 - core, z, c)

    def weight(i):
        if i < 4:
            return pltpu.make_async_copy(wa_hbm.at[i], wa.at[i], w_sem.at[i])
        if i == 4:
            return pltpu.make_async_copy(wu_hbm, wu, w_sem.at[4])
        return pltpu.make_async_copy(wd_hbm, wd, w_sem.at[5])

    for i in (1, 0, 2, 3, 4, 5):
        weight(i).start()

    barrier = pltpu.get_barrier_semaphore()
    for step in SEQ_STEPS:
        pl.semaphore_signal(barrier, inc=1, device_id=seq_peer(step)[0], device_id_type=MESH)
    for step in DEPTH_STEPS:
        pl.semaphore_signal(barrier, inc=1, device_id=depth_peer(step)[0], device_id_type=MESH)
    pl.semaphore_signal(barrier, inc=1, device_id=partner, device_id_type=MESH)
    pl.semaphore_wait(barrier, 15)

    xs[...] = x_ref[...]

    def remote(src, dst, ss, rs, dev):
        return pltpu.make_async_remote_copy(
            src_ref=src, dst_ref=dst, send_sem=ss, recv_sem=rs, device_id=dev, device_id_type=MESH
        )

    gain_swap = remote(coarse_ref, gains.at[8], csend_sem.at[0], crecv_sem.at[0], partner)
    gain_swap.start()

    def gain_copy(i, step):
        dev, _ = depth_peer(step)
        return remote(
            gains.at[9], gains.at[chip], dsend_sem.at[2, i], drecv_sem.at[2, chip], dev
        )

    def seq_copy(p, kind, i, step):
        dev, dest = seq_peer(step)
        src = (stage.at[0, dest], stage.at[1, dest], stage_v.at[dest], stage_a.at[dest])[kind]
        dst = (kr, qr, vr, ar)[kind].at[p, me]
        return remote(src, dst, send_sem.at[kind, i], recv_sem.at[p, kind, me], dev)

    def seq_arrival(p, kind, i, step):
        who = seq_from(step)
        dst = (kr, qr, vr, ar)[kind].at[p, who]
        dev, _ = seq_peer(step)
        return remote(dst, dst, send_sem.at[kind, i], recv_sem.at[p, kind, who], dev)

    def send_all(p, kind):
        for i, step in enumerate(SEQ_STEPS):
            seq_copy(p, kind, i, step).start()

    def wait_all(p, kind):
        for i, step in enumerate(SEQ_STEPS):
            seq_arrival(p, kind, i, step).wait_recv()

    def one_pass(p, carry):
        first = p == 0
        nb[...] = rms(xs[...].astype(jnp.float32), gain_ref[0:1]).astype(jnp.bfloat16)

        def project(which, store):
            @pl.when(first)
            def _():
                weight(which).wait()

            def tile(t, carry):
                cols = pl.ds(pl.multiple_of(t * 256, 256), 256)
                store(t, dot(nb[...], wa[which, :, cols]).astype(jnp.bfloat16))
                return carry

            lax.fori_loop(0, 4, tile, 0)

        def store_k(t, r):
            stage[0, 2 * t] = r[:, :LANES]
            stage[0, 2 * t + 1] = r[:, LANES:]

        def store_q(t, r):
            r = r * jnp.bfloat16(0.125)
            stage[1, 2 * t] = r[:, :LANES]
            stage[1, 2 * t + 1] = r[:, LANES:]

        def store_v(t, r):
            r = r.T
            stage_v[2 * t] = r[:LANES]
            stage_v[2 * t + 1] = r[LANES:]

        project(1, store_k)
        send_all(p, K)
        kr[p, me] = stage[0, me]
        project(0, store_q)
        send_all(p, Q)
        qr[p, me] = stage[1, me]
        project(2, store_v)
        send_all(p, V)
        vr[p, me] = stage_v[me]

        @pl.when(first)
        def _():
            gain_swap.wait()
            gains[9] = coarse_ref[...] * gains[8]
            gains[chip] = gains[9]
            for i, step in enumerate(DEPTH_STEPS):
                gain_copy(i, step).start()

            def build(qb, carry):
                doc_q = doc_ref[qb]

                def inner(d, carry):
                    kb = qb - d
                    doc_k = jnp.broadcast_to(doc_ref[kb], (LANES, ROWS)).T
                    doc_k = jnp.concatenate([doc_k, doc_k], axis=1)
                    kpos = lax.broadcasted_iota(jnp.int32, (ROWS, ROWS), 0) - d * ROWS
                    qpos = lax.broadcasted_iota(jnp.int32, (ROWS, ROWS), 1)
                    ok = (kpos <= qpos) & (doc_k == doc_q)
                    mask[qb * SPAN + d] = jnp.where(ok, jnp.inf, 0.0).astype(jnp.bfloat16)
                    return carry

                return lax.fori_loop(0, jnp.minimum(qb, SPAN - 1) + 1, inner, carry)

            lax.fori_loop(0, GROUPS, build, 0)

        wait_all(p, K)
        wait_all(p, Q)

        def scores(qb, count):
            q = qr[p, qb]
            lane = lax.broadcasted_iota(jnp.int32, (ROWS, LANES), 1)
            parts = [
                jnp.where(lane < HEAD, q, jnp.zeros_like(q)),
                jnp.where(lane < HEAD, jnp.zeros_like(q), q),
            ]
            for d in range(count):
                keys = kr[p, qb - d]
                m = mask[qb * SPAN + d]
                for i in range(2):
                    s = lax.dot_general(keys, parts[i], NT, preferred_element_type=jnp.float32)
                    e = jnp.exp(s).astype(jnp.bfloat16)
                    prob[i, qb * SPAN + d] = jnp.minimum(e, m)

        for qb in range(SPAN - 1):
            scores(qb, qb + 1)

        def late(qb, carry):
            scores(qb, SPAN)
            return carry

        lax.fori_loop(SPAN - 1, GROUPS, late, 0)

        wait_all(p, V)
        ones = jnp.ones((16, ROWS), jnp.bfloat16)

        def attend(qb):
            def inner(d, carry):
                vt = vr[p, qb - d]
                out = []
                for i in range(2):
                    lhs = jnp.concatenate([vt[i * HEAD:(i + 1) * HEAD], ones], axis=0)
                    out.append(carry[i] + dot(lhs, prob[i, qb * SPAN + d]))
                return tuple(out)

            start = jnp.zeros((HEAD + 16, ROWS), jnp.float32)
            nums = lax.fori_loop(0, jnp.minimum(qb, SPAN - 1) + 1, inner, (start, start))
            both = [n[:HEAD] / n[HEAD:HEAD + 1] for n in nums]
            return jnp.concatenate(both, axis=0).T.astype(jnp.bfloat16)

        for i, step in enumerate(SEQ_STEPS):
            _, dest = seq_peer(step)
            stage_a[dest] = attend(dest)
            seq_copy(p, A, i, step).start()
        ar[p, me] = attend(me)

        @pl.when(first)
        def _():
            weight(3).wait()

        wait_all(p, A)
        attended = jnp.concatenate([ar[p, j] for j in range(GROUPS)], axis=1)
        nb[...] = attended

        def project_out(t, carry):
            cols = pl.ds(pl.multiple_of(t * 256, 256), 256)
            mixed[:, cols] = xs[:, cols].astype(jnp.float32) + dot(nb[...], wa[3, :, cols])
            return carry

        lax.fori_loop(0, 4, project_out, 0)
        second[...] = rms(mixed[...], gain_ref[1:2]).astype(jnp.bfloat16)

        @pl.when(first)
        def _():
            weight(4).wait()
            weight(5).wait()

        def feed(t, carry):
            cols = pl.ds(pl.multiple_of(t * 512, 512), 512)
            hidden = jax.nn.gelu(dot(second[...], wu[:, cols])).astype(jnp.bfloat16)
            mixed[...] += dot(hidden, wd[cols, :])
            return carry

        lax.fori_loop(0, FF // 512, feed, 0)

        for kind in (K, Q, V, A):
            for i, step in enumerate(SEQ_STEPS):
                seq_copy(p, kind, i, step).wait_send()

        @pl.when(first)
        def _():
            exchange()

        return carry

    def depth_copy(stage_no, i, step):
        dev, dest = depth_peer(step)
        if stage_no == 0:
            src = comp.at[pl.ds(pl.multiple_of(dest * 16, 16), 16)]
            dst = depth_a.at[chip]
        else:
            src, dst = depth_u.at[dest], depth_r.at[chip]
        return remote(src, dst, dsend_sem.at[stage_no, i], drecv_sem.at[stage_no, chip], dev)

    def depth_arrival(stage_no, i, step):
        ph, py = lax.rem(h + step[0], 2), lax.rem(y + 4 - step[1], 4)
        who = 4 * ph + py
        dst = (depth_a, depth_r, gains)[stage_no].at[who]
        dev, _ = depth_peer(step)
        return remote(dst, dst, dsend_sem.at[stage_no, i], drecv_sem.at[stage_no, who], dev)

    def exchange():
        lead = jnp.where((h + y + core) == 0, 0.0, 1.0)
        gain = coarse_ref[...]
        a = mixed[...].astype(jnp.bfloat16).astype(jnp.float32)
        fine[...] = (a - (lead * gain) * x_ref[...].astype(jnp.float32)).astype(jnp.bfloat16)
        theirs = pl.ds(pl.multiple_of((1 - core) * 128, 128), 128)
        mine = pl.ds(pl.multiple_of(core * 128, 128), 128)
        swap = remote(fine.at[theirs], half_in, csend_sem.at[1], crecv_sem.at[1], partner)
        swap.start()
        swap.wait()
        is_low = core == 0
        own, other = fine[mine, :].astype(jnp.float32), half_in[...].astype(jnp.float32)
        low, high = jnp.where(is_low, own, other), jnp.where(is_low, other, own)
        gain_low = jnp.where(is_low, gain, gains[8])
        gain_high = jnp.where(is_low, gains[8], gain)
        comp[...] = (high + gain_high * low).astype(jnp.bfloat16)
        for i, step in enumerate(DEPTH_STEPS):
            depth_copy(0, i, step).start()
        depth_a[chip] = comp[pl.ds(pl.multiple_of(chip * 16, 16), 16), :]
        for i, step in enumerate(DEPTH_STEPS):
            gain_copy(i, step).wait_send()
            depth_arrival(2, i, step).wait_recv()
            depth_arrival(0, i, step).wait_recv()
        u = jnp.zeros((16, D), jnp.float32)
        for k in range(8):
            depth_u[k] = u.astype(jnp.bfloat16)
            u = depth_a[k].astype(jnp.float32) + gains[k] * u
        for i, step in enumerate(DEPTH_STEPS):
            depth_copy(1, i, step).start()
        depth_r[chip] = depth_u[chip]
        for i, step in enumerate(DEPTH_STEPS):
            depth_arrival(1, i, step).wait_recv()
            depth_copy(0, i, step).wait_send()
            depth_copy(1, i, step).wait_send()
        back = jnp.concatenate([depth_r[k] for k in range(8)], axis=0).astype(jnp.float32)
        own, other = fine[mine, :].astype(jnp.float32), half_in[...].astype(jnp.float32)
        low = jnp.where(is_low, own, other)
        after = low + gain_low * back
        given[...] = jnp.where(is_low, after, back).astype(jnp.bfloat16)
        give = remote(given, corrected.at[mine], csend_sem.at[2], crecv_sem.at[2], partner)
        give.start()
        keep = jnp.where(is_low, back, after).astype(jnp.bfloat16)
        xs[mine, :] = keep
        give.wait_send()
        remote(given, corrected.at[theirs], csend_sem.at[2], crecv_sem.at[2], partner).wait_recv()
        xs[theirs, :] = corrected[theirs, :]

        @pl.when((h + y + core) == 0)
        def _():
            xs[...] = x_ref[...]

    lax.fori_loop(0, 2, one_pass, 0)
    o_ref[...] = mixed[...].astype(jnp.bfloat16)


def on_device(interfaces, doc_ids, w_attn, w_up, w_down, norm_gains, coarse_gain):
    x = interfaces.reshape(ROWS, D)
    doc = doc_ids.astype(jnp.float32).reshape(GROUPS, 1, ROWS)
    bf, f32 = jnp.bfloat16, jnp.float32
    vmem = pl.BlockSpec(memory_space=pltpu.VMEM)
    hbm = pl.BlockSpec(memory_space=pl.ANY)
    out = pl.pallas_call(
        kernel,
        out_shape=jax.ShapeDtypeStruct((ROWS, D), bf),
        in_specs=[vmem] * 4 + [hbm] * 3,
        out_specs=vmem,
        scratch_shapes=[
            pltpu.VMEM((4, D, D), bf),
            pltpu.VMEM((D, FF), bf),
            pltpu.VMEM((FF, D), bf),
            pltpu.VMEM((ROWS, D), bf),
            pltpu.VMEM((ROWS, D), bf),
            pltpu.VMEM((2, GROUPS, ROWS, LANES), bf),
            pltpu.VMEM((GROUPS, LANES, ROWS), bf),
            pltpu.VMEM((2, GROUPS, ROWS, LANES), bf),
            pltpu.VMEM((2, GROUPS, ROWS, LANES), bf),
            pltpu.VMEM((2, GROUPS, LANES, ROWS), bf),
            pltpu.VMEM((GROUPS * SPAN, ROWS, ROWS), bf),
            pltpu.VMEM((2, GROUPS * SPAN, ROWS, ROWS), bf),
            pltpu.VMEM((GROUPS, ROWS, LANES), bf),
            pltpu.VMEM((2, GROUPS, ROWS, LANES), bf),
            pltpu.VMEM((ROWS, D), f32),
            pltpu.VMEM((ROWS, D), bf),
            pltpu.VMEM((8, 128), f32),
            pltpu.VMEM((10, 1, D), f32),
            pltpu.VMEM((ROWS, D), bf),
            pltpu.VMEM((128, D), bf),
            pltpu.VMEM((128, D), bf),
            pltpu.VMEM((8, 16, D), bf),
            pltpu.VMEM((8, 16, D), bf),
            pltpu.VMEM((8, 16, D), bf),
            pltpu.VMEM((128, D), bf),
            pltpu.VMEM((ROWS, D), bf),
            pltpu.SemaphoreType.DMA((6,)),
            pltpu.SemaphoreType.DMA((4, 7)),
            pltpu.SemaphoreType.DMA((2, 4, 8)),
            pltpu.SemaphoreType.DMA((3, 7)),
            pltpu.SemaphoreType.DMA((3, 8)),
            pltpu.SemaphoreType.DMA((3,)),
            pltpu.SemaphoreType.DMA((3,)),
        ],
        compiler_params=pltpu.CompilerParams(
            collective_id=0, has_side_effects=True, vmem_limit_bytes=60 * 2**20
        ),
        name="cycle",
    )(
        x,
        doc,
        norm_gains.reshape(2, D),
        coarse_gain.reshape(1, D),
        w_attn.reshape(4, D, D),
        w_up.reshape(D, FF),
        w_down.reshape(FF, D),
    )
    return out.reshape(1, 1, ROWS, D)


def solution(mesh):
    split = Mesh(
        mesh.devices.reshape(2, 4, 2, 4, 2), ("depth_0", "depth_1", "depth_2", "seq_0", "seq_1")
    )
    in_specs = (
        P(DEPTH, None, SEQ, None),
        P(),
        P(DEPTH, None, None, None, None),
        P(DEPTH, None, None, None),
        P(DEPTH, None, None, None),
        P(DEPTH, None, None, None),
        P(DEPTH, None),
    )
    out_specs = P(DEPTH, None, SEQ, None)
    return jax.shard_map(
        on_device, mesh=split, in_specs=in_specs, out_specs=out_specs, check_vma=False
    )
```

```python
import functools

import jax
import jax.numpy as jnp
from jax import lax
from jax.experimental import pallas as pl
from jax.experimental.pallas import tpu as pltpu
from jax.sharding import Mesh
from jax.sharding import PartitionSpec as P

D = 1024
FF = 4096
ROWS = 256
LANES = 128
HEAD = 64
GROUPS = 8
SPAN = 5
SEQ = ("seq_0", "seq_1")
DEPTH = ("depth_0", "depth_1", "depth_2")
MESH = pl.DeviceIdType.MESH
K, Q, V, A = 0, 1, 2, 4
NT = (((1,), (1,)), ((), ()))


def dot(a, b):
    return jnp.dot(a, b, preferred_element_type=jnp.float32)


def each(count, action):
    def body(i, carry):
        action(i)
        return carry

    lax.fori_loop(0, count, body, 0)


def row_step(u):
    return (2 - u) + lax.div(u, 2) * (7 - 2 * u)


def seq_step(i):
    u = lax.div(i, 2)
    return row_step(u), 1 - (i - 2 * u)


def depth_step(i):
    u = lax.div(i + 1, 4)
    return u, i + 1 - 4 * u


def gelu(x):
    inner = x * (x * x * (0.044715 * 0.7978845608028654) + 0.7978845608028654)
    part = 0.5 * x
    return part * jnp.tanh(inner) + part


def rms(value, gain):
    return value * lax.rsqrt(jnp.mean(value * value, axis=-1, keepdims=True) + 1e-05) * gain


def kernel(
    x_hbm, doc_hbm, gain_hbm, coarse_hbm, wa_hbm, wu_hbm, wd_hbm, o_ref,
    x_ref, doc_ref, gain_ref, coarse_ref, wa, wu, wd, xs, nb, stage, stage_v, kr, qr, vr, mask, prob, stage_a, ar, mixed, hidden,
    gains, fine, half_in, comp, depth_a, depth_u, depth_r, given, corrected,
    in_sem, w_sem, wide_sem, send_sem, recv_sem, g_sem, dsend_sem, drecv_sem, csend_sem, crecv_sem,
):
    h, y, core = (lax.axis_index(a) for a in DEPTH)
    z, c = (lax.axis_index(a) for a in SEQ)
    me = 2 * z + c
    chip = 4 * h + y
    partner = (h, y, 1 - core, z, c)

    def seq_peer(dz, dx):
        pz, pc = lax.rem(z + 4 + dz, 4), lax.rem(c + dx, 2)
        return (h, y, core, pz, pc), 2 * pz + pc

    def depth_peer(dh, dy):
        ph, py = lax.rem(h + dh, 2), lax.rem(y + 4 + dy, 4)
        return (ph, py, core, z, c), 4 * ph + py

    def remote(src, dst, ss, rs, dev):
        return pltpu.make_async_remote_copy(
            src_ref=src, dst_ref=dst, send_sem=ss, recv_sem=rs, device_id=dev, device_id_type=MESH
        )

    def tile_cols(n):
        return pl.ds(pl.multiple_of(lax.rem(z + row_step(n), 4) * 256, 256), 256)

    def narrow(which, n):
        cols = tile_cols(n)
        return pltpu.make_async_copy(
            wa_hbm.at[which, :, cols], wa.at[which, :, cols], w_sem.at[which, n]
        )

    def wide(i):
        src, dst = ((wu_hbm, wu), (wd_hbm, wd))[i]
        return pltpu.make_async_copy(src, dst, wide_sem.at[i])

    def wide_out(j):
        i = lax.rem(j, 2)
        rows = pl.ds(pl.multiple_of(j * HEAD, HEAD), HEAD)
        place = pl.ds(pl.multiple_of(i * 512 + lax.div(j, 2) * HEAD, HEAD), HEAD)
        return pltpu.make_async_copy(wa_hbm.at[3, rows], wa.at[3, place], wide_sem.at[2])

    def wide_out_total():
        return pltpu.make_async_copy(wa_hbm.at[3], wa.at[3], wide_sem.at[2])

    def entry(i):
        src = (x_hbm, gain_hbm, x_hbm, doc_hbm, coarse_hbm)[i]
        dst = (xs, gain_ref, x_ref, doc_ref, coarse_ref)[i]
        return pltpu.make_async_copy(src, dst, in_sem.at[i])

    entry(0).start()
    entry(1).start()
    each(4, lambda n: narrow(1, n).start())

    barrier = pltpu.get_barrier_semaphore()

    def greet(dev):
        pl.semaphore_signal(barrier, inc=1, device_id=dev, device_id_type=MESH)

    each(7, lambda i: greet(seq_peer(*seq_step(i))[0]))
    each(7, lambda i: greet(depth_peer(*depth_step(i))[0]))
    greet(partner)
    entry(0).wait()
    entry(1).wait()
    each(4, lambda n: narrow(0, n).start())
    each(4, lambda n: narrow(2, n).start())
    for i in range(2, 5):
        entry(i).start()

    gain_swap = remote(coarse_ref, gains.at[8], csend_sem.at[2, 0], crecv_sem.at[2, 0], partner)

    def gain_copy(i):
        dev, _ = depth_peer(*depth_step(i))
        return remote(gains.at[9], gains.at[chip], g_sem.at[0], g_sem.at[1], dev)

    def gain_total():
        some = gains.at[pl.ds(0, 7)]
        return remote(some, some, g_sem.at[0], g_sem.at[1], partner)

    def seq_copy(p, kind, i):
        dev, dest = seq_peer(*seq_step(i))
        if kind == K:
            src, dst = stage.at[0, dest], kr.at[p, me]
        elif kind == Q:
            src, dst = stage.at[1, dest], qr.at[p, me]
        else:
            src, dst = stage_v.at[kind - V, dest], vr.at[p, kind - V, me]
        return remote(src, dst, send_sem.at[kind], recv_sem.at[p, kind], dev)

    def back_copy(p, i, dest):
        pz = lax.div(dest, 2)
        dev = (h, y, core, pz, dest - 2 * pz)
        return remote(
            stage_a.at[i, dest], ar.at[p, i, me], send_sem.at[A + i], recv_sem.at[p, A + i], dev
        )

    def total(p, kind):
        seven = pl.ds(0, 7)
        if kind == K:
            some = kr.at[p, seven]
        elif kind == Q:
            some = qr.at[p, seven]
        elif kind < A:
            some = vr.at[p, kind - V, seven]
        else:
            some = ar.at[p, kind - A, seven]
        return remote(some, some, send_sem.at[kind], recv_sem.at[p, kind], partner)

    lane = lax.broadcasted_iota(jnp.int32, (ROWS, LANES), 1)

    def one_pass(p, carry):
        first = p == 0
        nb[...] = rms(xs[...].astype(jnp.float32), gain_ref[0:1]).astype(jnp.bfloat16)

        def project(which, kind, store):
            def tile(u):
                @pl.when(first)
                def _():
                    narrow(which, u).wait()

                base = 2 * lax.rem(z + row_step(u), 4)
                store(base, dot(nb[...], wa[which, :, tile_cols(u)]).astype(jnp.bfloat16))
                if kind == K:

                    @pl.when(first & (u == 0))
                    def _():
                        pl.semaphore_wait(barrier, 15)

                if kind != V:
                    seq_copy(p, kind, 2 * u).start()

                    @pl.when(u < 3)
                    def _():
                        seq_copy(p, kind, 2 * u + 1).start()

            each(4, tile)
            if kind == V:
                each(7, lambda i: seq_copy(p, V, i).start())
                each(7, lambda i: seq_copy(p, V + 1, i).start())

        def store_k(base, r):
            stage[0, base] = r[:, :LANES]
            stage[0, base + 1] = r[:, LANES:]

        def store_q(base, r):
            r = r * jnp.bfloat16(0.125)
            stage[1, base] = r[:, :LANES]
            stage[1, base + 1] = r[:, LANES:]

        def store_v(base, r):
            r = r.T
            for j in range(2):
                for i in range(2):
                    stage_v[i, base + j] = r[j * LANES + i * HEAD:j * LANES + (i + 1) * HEAD]

        project(1, K, store_k)
        kr[p, me] = stage[0, me]
        project(0, Q, store_q)
        qr[p, me] = stage[1, me]
        project(2, V, store_v)
        for i in range(2):
            vr[p, i, me] = stage_v[i, me]

        @pl.when(first)
        def _():
            each(16, lambda j: wide_out(j).start())
            wide(0).start()
            wide(1).start()
            for i in range(2, 5):
                entry(i).wait()
            gain_swap.start()
            gain_swap.wait()
            gains[9] = coarse_ref[...] * gains[8]
            gains[chip] = gains[9]
            each(7, lambda i: gain_copy(i).start())

            def build(qb, carry):
                doc_q = doc_ref[qb].astype(jnp.float32)

                def inner(d, carry):
                    doc_k = doc_ref[qb - d].astype(jnp.float32)
                    doc_k = jnp.broadcast_to(doc_k, (LANES, ROWS)).T
                    doc_k = jnp.concatenate([doc_k, doc_k], axis=1)
                    kpos = lax.broadcasted_iota(jnp.int32, (ROWS, ROWS), 0) - d * ROWS
                    qpos = lax.broadcasted_iota(jnp.int32, (ROWS, ROWS), 1)
                    ok = (kpos <= qpos) & (doc_k == doc_q)
                    mask[qb * SPAN + d] = jnp.where(ok, jnp.inf, 0.0).astype(jnp.bfloat16)
                    return carry

                return lax.fori_loop(0, jnp.minimum(qb, SPAN - 1) + 1, inner, carry)

            lax.fori_loop(0, GROUPS, build, 0)

        total(p, K).wait_recv()
        total(p, Q).wait_recv()
        own = jnp.where(me >= 4, me - 4, jnp.where((me == 0) | (me == 3), 4, 5))

        def unit_of(t):
            unit = lax.rem(own + 1 + t, 6)
            paired = unit >= 4
            low = jnp.where(paired, unit - 4, unit + 4)
            high = jnp.where(paired, 3 - low, low)
            split = jnp.where(paired, low + 1, SPAN)
            return paired, low, high, split

        def weigh(t):
            _, low, high, split = unit_of(t)
            for j in range(SPAN):
                is_low = j < split
                qb = jnp.where(is_low, low, high)
                d = jnp.where(is_low, j, j - split)
                q = qr[p, qb]
                zero = jnp.zeros_like(q)
                parts = jnp.where(lane < HEAD, q, zero), jnp.where(lane < HEAD, zero, q)
                keys = kr[p, qb - d]
                m = mask[qb * SPAN + d]
                for i in range(2):
                    s = lax.dot_general(keys, parts[i], NT, preferred_element_type=jnp.float32)
                    e = jnp.exp(s).astype(jnp.bfloat16)
                    prob[t, i, pl.ds(j * ROWS, ROWS)] = jnp.minimum(e, m)

        each(6, weigh)

        def gather_values(i):
            total(p, V + i).wait_recv()

            def one(t):
                paired, low, high, split = unit_of(t)
                lhs = [[], [], [], []]
                for j in range(SPAN):
                    is_low = j < split
                    block = jnp.where(is_low, low - j, high - j + split)
                    v = vr[p, i, block]
                    ones = jnp.ones((16, ROWS), jnp.bfloat16)
                    lhs[0].append(jnp.where(is_low, v, 0))
                    lhs[1].append(jnp.where(is_low, ones, 0))
                    lhs[2].append(jnp.where(is_low, 0, v))
                    lhs[3].append(jnp.where(is_low, 0, ones))
                lhs = jnp.concatenate([jnp.concatenate(part, axis=1) for part in lhs], axis=0)
                n = dot(lhs, prob[t, i])

                def finish(side, qb):
                    base = side * (HEAD + 16)
                    out = n[base:base + HEAD] / n[base + HEAD:base + HEAD + 1]
                    stage_a[i, qb] = out.astype(jnp.bfloat16)

                    @pl.when(qb != me)
                    def _():
                        back_copy(p, i, qb).start()

                finish(0, low)

                @pl.when(paired)
                def _():
                    finish(1, high)

            each(6, one)
            ar[p, i, me] = stage_a[i, me]

        gather_values(0)
        gather_values(1)

        @pl.when(first)
        def _():
            wide_out_total().wait()

        def project_out(i):
            total(p, A + i).wait_recv()
            part = ar[p, i].reshape(512, ROWS).T
            for t in range(4):
                cols = pl.ds(t * 256, 256)
                before = xs[:, cols].astype(jnp.float32) if i == 0 else mixed[:, cols]
                mixed[:, cols] = before + dot(part, wa[3, pl.ds(i * 512, 512), cols])

        project_out(0)
        project_out(1)
        nb[...] = rms(mixed[...], gain_ref[1:2]).astype(jnp.bfloat16)

        @pl.when(first)
        def _():
            wide(0).wait()

        def expand(t):
            cols = pl.ds(pl.multiple_of(t * 1024, 1024), 1024)
            hidden[:, cols] = gelu(dot(nb[...], wu[:, cols])).astype(jnp.bfloat16)

        each(FF // 1024, expand)

        for kind in (K, Q, V, V + 1, A, A + 1):
            total(p, kind).wait_send()

        @pl.when(first)
        def _():
            wide(1).wait()

        def lower(t):
            @pl.when(t < 4)
            def _():
                cols = pl.ds(pl.multiple_of(t * 256, 256), 256)
                o_ref[:, cols] = (mixed[:, cols] + dot(hidden[...], wd[:, cols])).astype(
                    jnp.bfloat16
                )

            n = lax.div(t, 2)
            odd = t - 2 * n

            @pl.when(first & (odd == 1))
            def _():
                swap_out(n)

            @pl.when(first & (odd == 0) & (t > 0))
            def _():
                compose(n - 1)

        each(5, lower)

        @pl.when(first)
        def _():
            each(2, scan)
            each(2, hand_over)
            each(2, collect)

            @pl.when((h + y + core) == 0)
            def _():
                xs[...] = x_ref[...]

        return carry

    theirs = pl.ds(pl.multiple_of((1 - core) * 128, 128), 128)
    mine = pl.ds(pl.multiple_of(core * 128, 128), 128)
    is_low = core == 0

    def half(n):
        return pl.ds(pl.multiple_of(n * 512, 512), 512)

    def low_gain(n):
        return jnp.where(is_low, coarse_ref[:, half(n)], gains[8, :, half(n)])

    def high_gain(n):
        return jnp.where(is_low, gains[8, :, half(n)], coarse_ref[:, half(n)])

    def swap_copy(n):
        return remote(
            fine.at[n, theirs], half_in.at[n], csend_sem.at[0, n], crecv_sem.at[0, n], partner
        )

    def give_copy(n):
        return remote(
            given.at[n], corrected.at[n], csend_sem.at[1, n], crecv_sem.at[1, n], partner
        )

    def depth_copy(n, trip, i):
        step = depth_step(i)
        dev, dest = depth_peer(*step)
        if trip == 0:
            src = comp.at[n, pl.ds(pl.multiple_of(dest * 16, 16), 16)]
            dst = depth_a.at[n, chip]
        else:
            src, dst = depth_u.at[n, dest], depth_r.at[n, chip]
        return remote(src, dst, dsend_sem.at[n, trip], drecv_sem.at[n, trip], dev)

    def depth_total(n, trip):
        some = (depth_a, depth_r)[trip].at[n, pl.ds(0, 7)]
        return remote(some, some, dsend_sem.at[n, trip], drecv_sem.at[n, trip], partner)

    def swap_out(n):
        lead = jnp.where((h + y + core) == 0, 0.0, 1.0)
        a = o_ref[:, half(n)].astype(jnp.float32)
        b = (lead * coarse_ref[:, half(n)]) * x_ref[:, half(n)].astype(jnp.float32)
        fine[n] = (a - b).astype(jnp.bfloat16)
        swap_copy(n).start()

    def compose(n):
        @pl.when(n == 0)
        def _():
            gain_total().wait()

        swap_copy(n).wait()
        own, other = fine[n, mine, :].astype(jnp.float32), half_in[n].astype(jnp.float32)
        low, high = jnp.where(is_low, own, other), jnp.where(is_low, other, own)
        comp[n] = (high + high_gain(n) * low).astype(jnp.bfloat16)
        each(7, lambda i: depth_copy(n, 0, i).start())
        depth_a[n, chip] = comp[n, pl.ds(pl.multiple_of(chip * 16, 16), 16), :]

    def scan(n):
        depth_total(n, 0).wait_recv()
        u = jnp.zeros((16, 512), jnp.float32)
        for k in range(8):
            depth_u[n, k] = u.astype(jnp.bfloat16)
            u = depth_a[n, k].astype(jnp.float32) + gains[k, :, half(n)] * u
        each(7, lambda i: depth_copy(n, 1, i).start())
        depth_r[n, chip] = depth_u[n, chip]

    def hand_over(n):
        depth_total(n, 1).wait_recv()
        back = jnp.concatenate([depth_r[n, k] for k in range(8)], axis=0).astype(jnp.float32)
        own, other = fine[n, mine, :].astype(jnp.float32), half_in[n].astype(jnp.float32)
        after = jnp.where(is_low, own, other) + low_gain(n) * back
        given[n] = jnp.where(is_low, after, back).astype(jnp.bfloat16)
        give_copy(n).start()
        xs[mine, half(n)] = jnp.where(is_low, back, after).astype(jnp.bfloat16)

    def collect(n):
        depth_total(n, 0).wait_send()
        depth_total(n, 1).wait_send()
        give_copy(n).wait()
        xs[theirs, half(n)] = corrected[n]

    lax.fori_loop(0, 2, one_pass, 0)


def on_device(interfaces, doc_ids, w_attn, w_up, w_down, norm_gains, coarse_gain):
    x = interfaces.reshape(ROWS, D)
    doc = doc_ids.reshape(GROUPS, 1, ROWS)
    bf, f32 = jnp.bfloat16, jnp.float32
    vmem = pl.BlockSpec(memory_space=pltpu.VMEM)
    hbm = pl.BlockSpec(memory_space=pl.ANY)
    out = pl.pallas_call(
        kernel,
        out_shape=pltpu.VMEM((ROWS, D), bf),
        in_specs=[hbm] * 7,
        out_specs=vmem,
        scratch_shapes=[
            pltpu.VMEM((ROWS, D), bf),
            pltpu.VMEM((GROUPS, 1, ROWS), jnp.int32),
            pltpu.VMEM((2, D), f32),
            pltpu.VMEM((1, D), f32),
            pltpu.VMEM((4, D, D), bf),
            pltpu.VMEM((D, FF), bf),
            pltpu.VMEM((FF, D), bf),
            pltpu.VMEM((ROWS, D), bf),
            pltpu.VMEM((ROWS, D), bf),
            pltpu.VMEM((2, GROUPS, ROWS, LANES), bf),
            pltpu.VMEM((2, GROUPS, HEAD, ROWS), bf),
            pltpu.VMEM((2, GROUPS, ROWS, LANES), bf),
            pltpu.VMEM((2, GROUPS, ROWS, LANES), bf),
            pltpu.VMEM((2, 2, GROUPS, HEAD, ROWS), bf),
            pltpu.VMEM((GROUPS * SPAN, ROWS, ROWS), bf),
            pltpu.VMEM((6, 2, SPAN * ROWS, ROWS), bf),
            pltpu.VMEM((2, GROUPS, HEAD, ROWS), bf),
            pltpu.VMEM((2, 2, GROUPS, HEAD, ROWS), bf),
            pltpu.VMEM((ROWS, D), f32),
            pltpu.VMEM((ROWS, FF), bf),
            pltpu.VMEM((10, 1, D), f32),
            pltpu.VMEM((2, ROWS, 512), bf),
            pltpu.VMEM((2, 128, 512), bf),
            pltpu.VMEM((2, 128, 512), bf),
            pltpu.VMEM((2, 8, 16, 512), bf),
            pltpu.VMEM((2, 8, 16, 512), bf),
            pltpu.VMEM((2, 8, 16, 512), bf),
            pltpu.VMEM((2, 128, 512), bf),
            pltpu.VMEM((2, 128, 512), bf),
            pltpu.SemaphoreType.DMA((5,)),
            pltpu.SemaphoreType.DMA((3, 4)),
            pltpu.SemaphoreType.DMA((3,)),
            pltpu.SemaphoreType.DMA((6,)),
            pltpu.SemaphoreType.DMA((2, 6)),
            pltpu.SemaphoreType.DMA((2,)),
            pltpu.SemaphoreType.DMA((2, 2)),
            pltpu.SemaphoreType.DMA((2, 2)),
            pltpu.SemaphoreType.DMA((3, 2)),
            pltpu.SemaphoreType.DMA((3, 2)),
        ],
        compiler_params=pltpu.CompilerParams(
            collective_id=0, has_side_effects=True, vmem_limit_bytes=60 * 2**20
        ),
        name="cycle",
    )(
        x,
        doc,
        norm_gains.reshape(2, D),
        coarse_gain.reshape(1, D),
        w_attn.reshape(4, D, D),
        w_up.reshape(D, FF),
        w_down.reshape(FF, D),
    )
    return out.reshape(1, 1, ROWS, D)


def solution(mesh):
    split = Mesh(
        mesh.devices.reshape(2, 4, 2, 4, 2), ("depth_0", "depth_1", "depth_2", "seq_0", "seq_1")
    )
    in_specs = (
        P(DEPTH, None, SEQ, None),
        P(),
        P(DEPTH, None, None, None, None),
        P(DEPTH, None, None, None),
        P(DEPTH, None, None, None),
        P(DEPTH, None, None, None),
        P(DEPTH, None),
    )
    out_specs = P(DEPTH, None, SEQ, None)
    return jax.shard_map(
        on_device, mesh=split, in_specs=in_specs, out_specs=out_specs, check_vma=False
    )
```

```python
import functools

import jax
import jax.numpy as jnp
from jax import lax
from jax.experimental import pallas as pl
from jax.experimental.pallas import tpu as pltpu
from jax.sharding import Mesh
from jax.sharding import PartitionSpec as P

D = 1024
FF = 4096
ROWS = 256
LANES = 128
HEAD = 64
GROUPS = 8
SPAN = 5
SEQ = ("seq_0", "seq_1")
DEPTH = ("depth_0", "depth_1", "depth_2")
MESH = pl.DeviceIdType.MESH
K, Q, V, A = 0, 1, 2, 4
NT = (((1,), (1,)), ((), ()))


def dot(a, b):
    return jnp.dot(a, b, preferred_element_type=jnp.float32)


def each(count, action):
    def body(i, carry):
        action(i)
        return carry

    lax.fori_loop(0, count, body, 0)


def row_step(u):
    return (2 - u) + lax.div(u, 2) * (7 - 2 * u)


def seq_step(i):
    u = lax.div(i, 2)
    return row_step(u), 1 - (i - 2 * u)


def depth_step(i):
    u = lax.div(i + 1, 4)
    return u, i + 1 - 4 * u


def gelu(x):
    inner = x * (x * x * (0.044715 * 0.7978845608028654) + 0.7978845608028654)
    part = 0.5 * x
    return part * jnp.tanh(inner) + part


def rms(value, gain):
    return value * lax.rsqrt(jnp.mean(value * value, axis=-1, keepdims=True) + 1e-05) * gain


def kernel(
    x_hbm, doc_hbm, gain_hbm, coarse_hbm, wa_hbm, wu_hbm, wd_hbm, o_ref,
    x_ref, doc_ref, gain_ref, coarse_ref, wa, wu, wd, xs, nb, stage, stage_v, kr, qr, vr, mask, prob, stage_a, ar, mixed, hidden,
    gains, fine, half_in, comp, depth_a, depth_u, depth_r, given, corrected,
    in_sem, w_sem, wide_sem, send_sem, recv_sem, q_sem, g_sem, dsend_sem, drecv_sem, csend_sem, crecv_sem,
):
    h, y, core = (lax.axis_index(a) for a in DEPTH)
    z, c = (lax.axis_index(a) for a in SEQ)
    me = 2 * z + c
    chip = 4 * h + y
    partner = (h, y, 1 - core, z, c)

    def seq_peer(dz, dx):
        pz, pc = lax.rem(z + 4 + dz, 4), lax.rem(c + dx, 2)
        return (h, y, core, pz, pc), 2 * pz + pc

    def depth_peer(dh, dy):
        ph, py = lax.rem(h + dh, 2), lax.rem(y + 4 + dy, 4)
        return (ph, py, core, z, c), 4 * ph + py

    def remote(src, dst, ss, rs, dev):
        return pltpu.make_async_remote_copy(
            src_ref=src, dst_ref=dst, send_sem=ss, recv_sem=rs, device_id=dev, device_id_type=MESH
        )

    def tile_cols(n):
        return pl.ds(pl.multiple_of(lax.rem(z + row_step(n), 4) * 256, 256), 256)

    def narrow(which, n):
        cols = tile_cols(n)
        return pltpu.make_async_copy(
            wa_hbm.at[which, :, cols], wa.at[which, :, cols], w_sem.at[which, n]
        )

    def wide(i):
        src, dst = ((wu_hbm, wu), (wd_hbm, wd))[i]
        return pltpu.make_async_copy(src, dst, wide_sem.at[i])

    def wide_out(j):
        i = lax.rem(j, 2)
        rows = pl.ds(pl.multiple_of(j * HEAD, HEAD), HEAD)
        place = pl.ds(pl.multiple_of(i * 512 + lax.div(j, 2) * HEAD, HEAD), HEAD)
        return pltpu.make_async_copy(wa_hbm.at[3, rows], wa.at[3, place], wide_sem.at[2])

    def wide_out_total():
        return pltpu.make_async_copy(wa_hbm.at[3], wa.at[3], wide_sem.at[2])

    def entry(i):
        src = (x_hbm, gain_hbm, x_hbm, doc_hbm, coarse_hbm)[i]
        dst = (xs, gain_ref, x_ref, doc_ref, coarse_ref)[i]
        return pltpu.make_async_copy(src, dst, in_sem.at[i])

    entry(0).start()
    entry(1).start()
    each(4, lambda n: narrow(1, n).start())

    barrier = pltpu.get_barrier_semaphore()

    def greet(dev):
        pl.semaphore_signal(barrier, inc=1, device_id=dev, device_id_type=MESH)

    each(7, lambda i: greet(seq_peer(*seq_step(i))[0]))
    each(7, lambda i: greet(depth_peer(*depth_step(i))[0]))
    greet(partner)
    entry(0).wait()
    entry(1).wait()
    each(4, lambda n: narrow(0, n).start())
    each(4, lambda n: narrow(2, n).start())
    for i in range(2, 5):
        entry(i).start()

    gain_swap = remote(coarse_ref, gains.at[8], csend_sem.at[2, 0], crecv_sem.at[2, 0], partner)

    def gain_copy(i):
        dev, _ = depth_peer(*depth_step(i))
        return remote(gains.at[9], gains.at[chip], g_sem.at[0], g_sem.at[1], dev)

    def gain_total():
        some = gains.at[pl.ds(0, 7)]
        return remote(some, some, g_sem.at[0], g_sem.at[1], partner)

    def seq_copy(p, kind, i):
        dev, dest = seq_peer(*seq_step(i))
        if kind == K:
            src, dst = stage.at[0, dest], kr.at[p, me]
        elif kind == Q:
            src, dst = stage.at[1, dest], qr.at[p, me]
        else:
            src, dst = stage_v.at[kind - V, dest], vr.at[p, kind - V, me]
        got = q_sem.at[p, me] if kind == Q else recv_sem.at[p, kind]
        return remote(src, dst, send_sem.at[kind], got, dev)

    def query_arrival(p, who):
        dst = qr.at[p, who]
        return remote(dst, dst, send_sem.at[Q], q_sem.at[p, who], partner)

    def back_copy(p, i, dest):
        pz = lax.div(dest, 2)
        dev = (h, y, core, pz, dest - 2 * pz)
        return remote(
            stage_a.at[i, dest], ar.at[p, i, me], send_sem.at[A + i], recv_sem.at[p, A + i], dev
        )

    def total(p, kind):
        seven = pl.ds(0, 7)
        if kind == K:
            some = kr.at[p, seven]
        elif kind == Q:
            some = qr.at[p, seven]
        elif kind < A:
            some = vr.at[p, kind - V, seven]
        else:
            some = ar.at[p, kind - A, seven]
        return remote(some, some, send_sem.at[kind], recv_sem.at[p, kind], partner)

    lane = lax.broadcasted_iota(jnp.int32, (ROWS, LANES), 1)

    def one_pass(p, carry):
        first = p == 0
        nb[...] = rms(xs[...].astype(jnp.float32), gain_ref[0:1]).astype(jnp.bfloat16)

        def project(which, kind, store):
            def tile(u):
                @pl.when(first)
                def _():
                    narrow(which, u).wait()

                base = 2 * lax.rem(z + row_step(u), 4)
                store(base, dot(nb[...], wa[which, :, tile_cols(u)]).astype(jnp.bfloat16))
                if kind == K:

                    @pl.when(first & (u == 0))
                    def _():
                        pl.semaphore_wait(barrier, 15)

                if kind != V:
                    seq_copy(p, kind, 2 * u).start()

                    @pl.when(u < 3)
                    def _():
                        seq_copy(p, kind, 2 * u + 1).start()

            each(4, tile)

        def store_k(base, r):
            stage[0, base] = r[:, :LANES]
            stage[0, base + 1] = r[:, LANES:]

        def store_q(base, r):
            r = r * jnp.bfloat16(0.125)
            stage[1, base] = r[:, :LANES]
            stage[1, base + 1] = r[:, LANES:]

        def store_v(base, r):
            r = r.T
            for j in range(2):
                for i in range(2):
                    stage_v[i, base + j] = r[j * LANES + i * HEAD:j * LANES + (i + 1) * HEAD]

        project(1, K, store_k)
        kr[p, me] = stage[0, me]
        project(0, Q, store_q)
        qr[p, me] = stage[1, me]
        project(2, V, store_v)
        each(7, lambda i: seq_copy(p, V, i).start())
        each(7, lambda i: seq_copy(p, V + 1, i).start())
        for i in range(2):
            vr[p, i, me] = stage_v[i, me]

        @pl.when(first)
        def _():
            each(16, lambda j: wide_out(j).start())
            wide(0).start()
            wide(1).start()
            for i in range(2, 5):
                entry(i).wait()
            gain_swap.start()
            gain_swap.wait()
            gains[9] = coarse_ref[...] * gains[8]
            gains[chip] = gains[9]
            each(7, lambda i: gain_copy(i).start())

            def build(qb, carry):
                doc_q = doc_ref[qb].astype(jnp.float32)

                def inner(d, carry):
                    doc_k = doc_ref[qb - d].astype(jnp.float32)
                    doc_k = jnp.broadcast_to(doc_k, (LANES, ROWS)).T
                    doc_k = jnp.concatenate([doc_k, doc_k], axis=1)
                    kpos = lax.broadcasted_iota(jnp.int32, (ROWS, ROWS), 0) - d * ROWS
                    qpos = lax.broadcasted_iota(jnp.int32, (ROWS, ROWS), 1)
                    ok = (kpos <= qpos) & (doc_k == doc_q)
                    mask[qb * SPAN + d] = jnp.where(ok, jnp.inf, 0.0).astype(jnp.bfloat16)
                    return carry

                return lax.fori_loop(0, jnp.minimum(qb, SPAN - 1) + 1, inner, carry)

            lax.fori_loop(0, GROUPS, build, 0)

        total(p, K).wait_recv()
        own = jnp.where(me >= 4, me - 4, jnp.where((me == 0) | (me == 3), 4, 5))

        def unit_of(t):
            g = lax.div(t, 2)
            near = jnp.where((z == 1) | (z == 2), 0, 2)
            full = jnp.where(lax.rem(g + z, 2) == lax.rem(z, 2), near, 2 - near)
            late = jnp.where(g == 1, near, 2 - near)
            base = jnp.where(
                z < 2,
                jnp.where(g == 0, 4, late),
                jnp.where(g == 2, 4, full),
            )
            unit = base + lax.rem(own + t, 2)
            paired = unit >= 4
            low = jnp.where(paired, unit - 4, unit + 4)
            high = jnp.where(paired, 3 - low, low)
            split = jnp.where(paired, low + 1, SPAN)
            return paired, low, high, split

        def weigh(t):
            paired, low, high, split = unit_of(t)

            @pl.when(low != me)
            def _():
                query_arrival(p, low).wait_recv()

            @pl.when(paired & (high != me))
            def _():
                query_arrival(p, high).wait_recv()

            for j in range(SPAN):
                is_low = j < split
                qb = jnp.where(is_low, low, high)
                d = jnp.where(is_low, j, j - split)
                q = qr[p, qb]
                zero = jnp.zeros_like(q)
                parts = jnp.where(lane < HEAD, q, zero), jnp.where(lane < HEAD, zero, q)
                keys = kr[p, qb - d]
                m = mask[qb * SPAN + d]
                for i in range(2):
                    s = lax.dot_general(keys, parts[i], NT, preferred_element_type=jnp.float32)
                    e = jnp.exp(s).astype(jnp.bfloat16)
                    prob[t, i, pl.ds(j * ROWS, ROWS)] = jnp.minimum(e, m)

        each(6, weigh)

        def gather_values(i):
            total(p, V + i).wait_recv()

            def combine(t):
                _, low, high, split = unit_of(t)
                lhs = [[], [], [], []]
                for j in range(SPAN):
                    is_low = j < split
                    block = jnp.where(is_low, low - j, high - j + split)
                    v = vr[p, i, block]
                    ones = jnp.ones((16, ROWS), jnp.bfloat16)
                    lhs[0].append(jnp.where(is_low, v, 0))
                    lhs[1].append(jnp.where(is_low, ones, 0))
                    lhs[2].append(jnp.where(is_low, 0, v))
                    lhs[3].append(jnp.where(is_low, 0, ones))
                lhs = jnp.concatenate([jnp.concatenate(part, axis=1) for part in lhs], axis=0)
                return dot(lhs, prob[t, i])

            def finish(n, side, qb):
                base = side * (HEAD + 16)
                out = n[base:base + HEAD] / n[base + HEAD:base + HEAD + 1]
                stage_a[i, qb] = out.astype(jnp.bfloat16)

                @pl.when(qb != me)
                def _():
                    back_copy(p, i, qb).start()

            def two(s):
                units = (5 - 2 * s, 4 - 2 * s)
                sums = [combine(t) for t in units]
                for t, n in zip(units, sums):
                    paired, low, high, _ = unit_of(t)
                    finish(n, 0, low)

                    @pl.when(paired)
                    def _():
                        finish(n, 1, high)

            each(3, two)
            ar[p, i, me] = stage_a[i, me]

        gather_values(0)
        gather_values(1)

        @pl.when(first)
        def _():
            wide_out_total().wait()

        def project_out(i):
            total(p, A + i).wait_recv()
            part = ar[p, i].reshape(512, ROWS).T
            for t in range(4):
                cols = pl.ds(t * 256, 256)
                before = xs[:, cols].astype(jnp.float32) if i == 0 else mixed[:, cols]
                mixed[:, cols] = before + dot(part, wa[3, pl.ds(i * 512, 512), cols])

        project_out(0)
        project_out(1)
        nb[...] = rms(mixed[...], gain_ref[1:2]).astype(jnp.bfloat16)

        @pl.when(first)
        def _():
            wide(0).wait()

        def expand(t):
            cols = pl.ds(pl.multiple_of(t * 2048, 2048), 2048)
            hidden[:, cols] = gelu(dot(nb[...], wu[:, cols])).astype(jnp.bfloat16)

        each(FF // 2048, expand)

        for kind in (K, Q, V, V + 1, A, A + 1):
            total(p, kind).wait_send()

        @pl.when(first)
        def _():
            wide(1).wait()

        def lower(t):
            @pl.when(t < 4)
            def _():
                cols = pl.ds(pl.multiple_of(t * 256, 256), 256)
                o_ref[:, cols] = (mixed[:, cols] + dot(hidden[...], wd[:, cols])).astype(
                    jnp.bfloat16
                )

            @pl.when(t < 4)
            def _():
                swap_out(t)

            @pl.when(t > 0)
            def _():
                compose(t - 1)

        @pl.when(first)
        def _():
            each(5, lower)

        @pl.when(p == 1)
        def _():
            o_ref[...] = (mixed[...] + dot(hidden[...], wd[...])).astype(jnp.bfloat16)

        @pl.when(first)
        def _():
            each(4, scan)
            each(4, hand_over)
            each(4, collect)

            @pl.when((h + y + core) == 0)
            def _():
                xs[...] = x_ref[...]

        return carry

    theirs = pl.ds(pl.multiple_of((1 - core) * 128, 128), 128)
    mine = pl.ds(pl.multiple_of(core * 128, 128), 128)
    is_low = core == 0

    def half(n):
        return pl.ds(pl.multiple_of(n * 256, 256), 256)

    def low_gain(n):
        return jnp.where(is_low, coarse_ref[:, half(n)], gains[8, :, half(n)])

    def high_gain(n):
        return jnp.where(is_low, gains[8, :, half(n)], coarse_ref[:, half(n)])

    def swap_copy(n):
        return remote(
            fine.at[n, theirs], half_in.at[n], csend_sem.at[0, n], crecv_sem.at[0, n], partner
        )

    def give_copy(n):
        return remote(
            given.at[n], corrected.at[n], csend_sem.at[1, n], crecv_sem.at[1, n], partner
        )

    def depth_copy(n, trip, i):
        step = depth_step(i)
        dev, dest = depth_peer(*step)
        if trip == 0:
            src = comp.at[n, pl.ds(pl.multiple_of(dest * 16, 16), 16)]
            dst = depth_a.at[n, chip]
        else:
            src, dst = depth_u.at[n, dest], depth_r.at[n, chip]
        return remote(src, dst, dsend_sem.at[n, trip], drecv_sem.at[n, trip], dev)

    def depth_total(n, trip):
        some = (depth_a, depth_r)[trip].at[n, pl.ds(0, 7)]
        return remote(some, some, dsend_sem.at[n, trip], drecv_sem.at[n, trip], partner)

    def swap_out(n):
        lead = jnp.where((h + y + core) == 0, 0.0, 1.0)
        a = o_ref[:, half(n)].astype(jnp.float32)
        b = (lead * coarse_ref[:, half(n)]) * x_ref[:, half(n)].astype(jnp.float32)
        fine[n] = (a - b).astype(jnp.bfloat16)
        swap_copy(n).start()

    def compose(n):
        @pl.when(n == 0)
        def _():
            gain_total().wait()

        swap_copy(n).wait()
        own, other = fine[n, mine, :].astype(jnp.float32), half_in[n].astype(jnp.float32)
        low, high = jnp.where(is_low, own, other), jnp.where(is_low, other, own)
        comp[n] = (high + high_gain(n) * low).astype(jnp.bfloat16)
        each(7, lambda i: depth_copy(n, 0, i).start())
        depth_a[n, chip] = comp[n, pl.ds(pl.multiple_of(chip * 16, 16), 16), :]

    def scan(n):
        depth_total(n, 0).wait_recv()
        u = jnp.zeros((16, 256), jnp.float32)
        for k in range(8):
            depth_u[n, k] = u.astype(jnp.bfloat16)
            u = depth_a[n, k].astype(jnp.float32) + gains[k, :, half(n)] * u
        each(7, lambda i: depth_copy(n, 1, i).start())
        depth_r[n, chip] = depth_u[n, chip]

    def hand_over(n):
        depth_total(n, 1).wait_recv()
        back = jnp.concatenate([depth_r[n, k] for k in range(8)], axis=0).astype(jnp.float32)
        own, other = fine[n, mine, :].astype(jnp.float32), half_in[n].astype(jnp.float32)
        after = jnp.where(is_low, own, other) + low_gain(n) * back
        given[n] = jnp.where(is_low, after, back).astype(jnp.bfloat16)
        give_copy(n).start()
        xs[mine, half(n)] = jnp.where(is_low, back, after).astype(jnp.bfloat16)

    def collect(n):
        depth_total(n, 0).wait_send()
        depth_total(n, 1).wait_send()
        give_copy(n).wait()
        xs[theirs, half(n)] = corrected[n]

    lax.fori_loop(0, 2, one_pass, 0)


def on_device(interfaces, doc_ids, w_attn, w_up, w_down, norm_gains, coarse_gain):
    x = interfaces.reshape(ROWS, D)
    doc = doc_ids.reshape(GROUPS, 1, ROWS)
    bf, f32 = jnp.bfloat16, jnp.float32
    vmem = pl.BlockSpec(memory_space=pltpu.VMEM)
    hbm = pl.BlockSpec(memory_space=pl.ANY)
    out = pl.pallas_call(
        kernel,
        out_shape=pltpu.VMEM((ROWS, D), bf),
        in_specs=[hbm] * 7,
        out_specs=vmem,
        scratch_shapes=[
            pltpu.VMEM((ROWS, D), bf),
            pltpu.VMEM((GROUPS, 1, ROWS), jnp.int32),
            pltpu.VMEM((2, D), f32),
            pltpu.VMEM((1, D), f32),
            pltpu.VMEM((4, D, D), bf),
            pltpu.VMEM((D, FF), bf),
            pltpu.VMEM((FF, D), bf),
            pltpu.VMEM((ROWS, D), bf),
            pltpu.VMEM((ROWS, D), bf),
            pltpu.VMEM((2, GROUPS, ROWS, LANES), bf),
            pltpu.VMEM((2, GROUPS, HEAD, ROWS), bf),
            pltpu.VMEM((2, GROUPS, ROWS, LANES), bf),
            pltpu.VMEM((2, GROUPS, ROWS, LANES), bf),
            pltpu.VMEM((2, 2, GROUPS, HEAD, ROWS), bf),
            pltpu.VMEM((GROUPS * SPAN, ROWS, ROWS), bf),
            pltpu.VMEM((6, 2, SPAN * ROWS, ROWS), bf),
            pltpu.VMEM((2, GROUPS, HEAD, ROWS), bf),
            pltpu.VMEM((2, 2, GROUPS, HEAD, ROWS), bf),
            pltpu.VMEM((ROWS, D), f32),
            pltpu.VMEM((ROWS, FF), bf),
            pltpu.VMEM((10, 1, D), f32),
            pltpu.VMEM((4, ROWS, 256), bf),
            pltpu.VMEM((4, 128, 256), bf),
            pltpu.VMEM((4, 128, 256), bf),
            pltpu.VMEM((4, 8, 16, 256), bf),
            pltpu.VMEM((4, 8, 16, 256), bf),
            pltpu.VMEM((4, 8, 16, 256), bf),
            pltpu.VMEM((4, 128, 256), bf),
            pltpu.VMEM((4, 128, 256), bf),
            pltpu.SemaphoreType.DMA((5,)),
            pltpu.SemaphoreType.DMA((3, 4)),
            pltpu.SemaphoreType.DMA((3,)),
            pltpu.SemaphoreType.DMA((6,)),
            pltpu.SemaphoreType.DMA((2, 6)),
            pltpu.SemaphoreType.DMA((2, 8)),
            pltpu.SemaphoreType.DMA((2,)),
            pltpu.SemaphoreType.DMA((4, 2)),
            pltpu.SemaphoreType.DMA((4, 2)),
            pltpu.SemaphoreType.DMA((3, 4)),
            pltpu.SemaphoreType.DMA((3, 4)),
        ],
        compiler_params=pltpu.CompilerParams(
            collective_id=0, has_side_effects=True, vmem_limit_bytes=60 * 2**20
        ),
        name="cycle",
    )(
        x,
        doc,
        norm_gains.reshape(2, D),
        coarse_gain.reshape(1, D),
        w_attn.reshape(4, D, D),
        w_up.reshape(D, FF),
        w_down.reshape(FF, D),
    )
    return out.reshape(1, 1, ROWS, D)


def solution(mesh):
    split = Mesh(
        mesh.devices.reshape(2, 4, 2, 4, 2), ("depth_0", "depth_1", "depth_2", "seq_0", "seq_1")
    )
    in_specs = (
        P(DEPTH, None, SEQ, None),
        P(),
        P(DEPTH, None, None, None, None),
        P(DEPTH, None, None, None),
        P(DEPTH, None, None, None),
        P(DEPTH, None, None, None),
        P(DEPTH, None),
    )
    out_specs = P(DEPTH, None, SEQ, None)
    return jax.shard_map(
        on_device, mesh=split, in_specs=in_specs, out_specs=out_specs, check_vma=False
    )
```

```python
import functools

import jax
import jax.numpy as jnp
from jax import lax
from jax.experimental import pallas as pl
from jax.experimental.pallas import tpu as pltpu
from jax.sharding import Mesh
from jax.sharding import PartitionSpec as P

D = 1024
FF = 4096
ROWS = 256
LANES = 128
HEAD = 64
GROUPS = 8
SPAN = 5
SEQ = ("seq_0", "seq_1")
DEPTH = ("depth_0", "depth_1", "depth_2")
MESH = pl.DeviceIdType.MESH
K, Q, V, A = 0, 1, 2, 4
NT = (((1,), (1,)), ((), ()))


def dot(a, b):
    return jnp.dot(a, b, preferred_element_type=jnp.float32)


def each(count, action):
    def body(i, carry):
        action(i)
        return carry

    lax.fori_loop(0, count, body, 0)


def row_step(u):
    return (2 - u) + lax.div(u, 2) * (7 - 2 * u)


def seq_step(i):
    u = lax.div(i, 2)
    return row_step(u), 1 - (i - 2 * u)


def depth_step(i):
    u = lax.div(i, 4)
    return 1 - u, row_step(i - 4 * u)


def gelu(x):
    inner = x * (x * x * (0.044715 * 0.7978845608028654) + 0.7978845608028654)
    part = 0.5 * x
    return part * jnp.tanh(inner) + part


def rms(value, gain):
    return value * lax.rsqrt(jnp.mean(value * value, axis=-1, keepdims=True) + 1e-05) * gain


def kernel(
    x_hbm, doc_hbm, gain_hbm, coarse_hbm, wa_hbm, wu_hbm, wd_hbm, o_ref,
    x_ref, doc_ref, gain_ref, coarse_ref, wa, wu, wd, xs, nb, stage, stage_v, kr, qr, vr, mask, prob, stage_a, ar, mixed, hidden,
    gains, fine, half_in, comp, depth_a, depth_u, depth_r, given, corrected,
    in_sem, w_sem, wide_sem, send_sem, recv_sem, q_sem, g_sem, dsend_sem, drecv_sem, csend_sem, crecv_sem,
):
    h, y, core = (lax.axis_index(a) for a in DEPTH)
    z, c = (lax.axis_index(a) for a in SEQ)
    me = 2 * z + c
    chip = 4 * h + y
    partner = (h, y, 1 - core, z, c)

    def seq_peer(dz, dx):
        pz, pc = lax.rem(z + 4 + dz, 4), lax.rem(c + dx, 2)
        return (h, y, core, pz, pc), 2 * pz + pc

    def depth_peer(dh, dy):
        ph, py = lax.rem(h + dh, 2), lax.rem(y + 4 + dy, 4)
        return (ph, py, core, z, c), 4 * ph + py

    def remote(src, dst, ss, rs, dev):
        return pltpu.make_async_remote_copy(
            src_ref=src, dst_ref=dst, send_sem=ss, recv_sem=rs, device_id=dev, device_id_type=MESH
        )

    def tile_cols(n):
        return pl.ds(pl.multiple_of(lax.rem(z + row_step(n), 4) * 256, 256), 256)

    def narrow(which, n):
        cols = tile_cols(n)
        return pltpu.make_async_copy(
            wa_hbm.at[which, :, cols], wa.at[which, :, cols], w_sem.at[which, n]
        )

    def wide(i):
        src, dst = ((wu_hbm, wu), (wd_hbm, wd))[i]
        return pltpu.make_async_copy(src, dst, wide_sem.at[i])

    def wide_out(j):
        i = lax.rem(j, 2)
        rows = pl.ds(pl.multiple_of(j * HEAD, HEAD), HEAD)
        place = pl.ds(pl.multiple_of(i * 512 + lax.div(j, 2) * HEAD, HEAD), HEAD)
        return pltpu.make_async_copy(wa_hbm.at[3, rows], wa.at[3, place], wide_sem.at[2])

    def wide_out_total():
        return pltpu.make_async_copy(wa_hbm.at[3], wa.at[3], wide_sem.at[2])

    def entry(i):
        src = (x_hbm, gain_hbm, x_hbm, doc_hbm, coarse_hbm)[i]
        dst = (xs, gain_ref, x_ref, doc_ref, coarse_ref)[i]
        return pltpu.make_async_copy(src, dst, in_sem.at[i])

    entry(0).start()
    entry(1).start()
    each(4, lambda n: narrow(1, n).start())

    barrier = pltpu.get_barrier_semaphore()

    def greet(dev):
        pl.semaphore_signal(barrier, inc=1, device_id=dev, device_id_type=MESH)

    each(7, lambda i: greet(seq_peer(*seq_step(i))[0]))
    each(7, lambda i: greet(depth_peer(*depth_step(i))[0]))
    greet(partner)
    entry(0).wait()
    entry(1).wait()
    each(4, lambda n: narrow(0, n).start())
    each(4, lambda n: narrow(2, n).start())
    for i in range(2, 5):
        entry(i).start()

    gain_swap = remote(coarse_ref, gains.at[8], csend_sem.at[2, 0], crecv_sem.at[2, 0], partner)

    def gain_copy(i):
        dev, _ = depth_peer(*depth_step(i))
        return remote(gains.at[9], gains.at[chip], g_sem.at[0], g_sem.at[1], dev)

    def gain_total():
        some = gains.at[pl.ds(0, 7)]
        return remote(some, some, g_sem.at[0], g_sem.at[1], partner)

    def seq_copy(p, kind, i):
        dev, dest = seq_peer(*seq_step(i))
        if kind == K:
            src, dst = stage.at[0, dest], kr.at[p, me]
        elif kind == Q:
            src, dst = stage.at[1, dest], qr.at[p, me]
        else:
            src, dst = stage_v.at[kind - V, dest], vr.at[p, kind - V, me]
        got = q_sem.at[p, me] if kind == Q else recv_sem.at[p, kind]
        return remote(src, dst, send_sem.at[kind], got, dev)

    def query_arrival(p, who):
        dst = qr.at[p, who]
        return remote(dst, dst, send_sem.at[Q], q_sem.at[p, who], partner)

    def back_copy(p, i, dest):
        pz = lax.div(dest, 2)
        dev = (h, y, core, pz, dest - 2 * pz)
        return remote(
            stage_a.at[i, dest], ar.at[p, i, me], send_sem.at[A + i], recv_sem.at[p, A + i], dev
        )

    def total(p, kind):
        seven = pl.ds(0, 7)
        if kind == K:
            some = kr.at[p, seven]
        elif kind == Q:
            some = qr.at[p, seven]
        elif kind < A:
            some = vr.at[p, kind - V, seven]
        else:
            some = ar.at[p, kind - A, seven]
        return remote(some, some, send_sem.at[kind], recv_sem.at[p, kind], partner)

    lane = lax.broadcasted_iota(jnp.int32, (ROWS, LANES), 1)

    def one_pass(p, carry):
        first = p == 0
        nb[...] = rms(xs[...].astype(jnp.float32), gain_ref[0:1]).astype(jnp.bfloat16)

        def project(which, kind, store):
            def tile(u):
                @pl.when(first)
                def _():
                    narrow(which, u).wait()

                base = 2 * lax.rem(z + row_step(u), 4)
                store(base, dot(nb[...], wa[which, :, tile_cols(u)]).astype(jnp.bfloat16))
                if kind == K:

                    @pl.when(first & (u == 0))
                    def _():
                        pl.semaphore_wait(barrier, 15)

                if kind != V:
                    seq_copy(p, kind, 2 * u).start()

                    @pl.when(u < 3)
                    def _():
                        seq_copy(p, kind, 2 * u + 1).start()

            each(4, tile)

        def store_k(base, r):
            stage[0, base] = r[:, :LANES]
            stage[0, base + 1] = r[:, LANES:]

        def store_q(base, r):
            r = r * jnp.bfloat16(0.125)
            stage[1, base] = r[:, :LANES]
            stage[1, base + 1] = r[:, LANES:]

        def store_v(base, r):
            r = r.T
            for j in range(2):
                for i in range(2):
                    stage_v[i, base + j] = r[j * LANES + i * HEAD:j * LANES + (i + 1) * HEAD]

        project(1, K, store_k)
        kr[p, me] = stage[0, me]
        project(0, Q, store_q)
        qr[p, me] = stage[1, me]
        project(2, V, store_v)
        each(7, lambda i: seq_copy(p, V, i).start())
        each(7, lambda i: seq_copy(p, V + 1, i).start())
        for i in range(2):
            vr[p, i, me] = stage_v[i, me]

        @pl.when(first)
        def _():
            each(16, lambda j: wide_out(j).start())
            wide(0).start()
            wide(1).start()
            for i in range(2, 5):
                entry(i).wait()
            gain_swap.start()
            gain_swap.wait()
            gains[9] = coarse_ref[...] * gains[8]
            gains[chip] = gains[9]
            each(7, lambda i: gain_copy(i).start())

            def build(qb, carry):
                doc_q = doc_ref[qb].astype(jnp.float32)

                def inner(d, carry):
                    doc_k = doc_ref[qb - d].astype(jnp.float32)
                    doc_k = jnp.broadcast_to(doc_k, (LANES, ROWS)).T
                    doc_k = jnp.concatenate([doc_k, doc_k], axis=1)
                    kpos = lax.broadcasted_iota(jnp.int32, (ROWS, ROWS), 0) - d * ROWS
                    qpos = lax.broadcasted_iota(jnp.int32, (ROWS, ROWS), 1)
                    ok = (kpos <= qpos) & (doc_k == doc_q)
                    mask[qb * SPAN + d] = jnp.where(ok, jnp.inf, 0.0).astype(jnp.bfloat16)
                    return carry

                return lax.fori_loop(0, jnp.minimum(qb, SPAN - 1) + 1, inner, carry)

            lax.fori_loop(0, GROUPS, build, 0)

        total(p, K).wait_recv()
        own = jnp.where(me >= 4, me - 4, jnp.where((me == 0) | (me == 3), 4, 5))

        def unit_of(t):
            g = lax.div(t, 2)
            near = jnp.where((z == 1) | (z == 2), 0, 2)
            full = jnp.where(lax.rem(g + z, 2) == lax.rem(z, 2), near, 2 - near)
            late = jnp.where(g == 1, near, 2 - near)
            base = jnp.where(
                z < 2,
                jnp.where(g == 0, 4, late),
                jnp.where(g == 2, 4, full),
            )
            unit = base + lax.rem(own + t, 2)
            paired = unit >= 4
            low = jnp.where(paired, unit - 4, unit + 4)
            high = jnp.where(paired, 3 - low, low)
            split = jnp.where(paired, low + 1, SPAN)
            return paired, low, high, split

        def weigh(t):
            paired, low, high, split = unit_of(t)

            @pl.when(low != me)
            def _():
                query_arrival(p, low).wait_recv()

            @pl.when(paired & (high != me))
            def _():
                query_arrival(p, high).wait_recv()

            for j in range(SPAN):
                is_low = j < split
                qb = jnp.where(is_low, low, high)
                d = jnp.where(is_low, j, j - split)
                q = qr[p, qb]
                zero = jnp.zeros_like(q)
                parts = jnp.where(lane < HEAD, q, zero), jnp.where(lane < HEAD, zero, q)
                keys = kr[p, qb - d]
                m = mask[qb * SPAN + d]
                for i in range(2):
                    s = lax.dot_general(keys, parts[i], NT, preferred_element_type=jnp.float32)
                    e = jnp.exp(s).astype(jnp.bfloat16)
                    prob[t, i, pl.ds(j * ROWS, ROWS)] = jnp.minimum(e, m)

        each(6, weigh)

        def gather_values(i):
            total(p, V + i).wait_recv()

            def combine(t):
                _, low, high, split = unit_of(t)
                lhs = [[], [], [], []]
                for j in range(SPAN):
                    is_low = j < split
                    block = jnp.where(is_low, low - j, high - j + split)
                    v = vr[p, i, block]
                    ones = jnp.ones((16, ROWS), jnp.bfloat16)
                    lhs[0].append(jnp.where(is_low, v, 0))
                    lhs[1].append(jnp.where(is_low, ones, 0))
                    lhs[2].append(jnp.where(is_low, 0, v))
                    lhs[3].append(jnp.where(is_low, 0, ones))
                lhs = jnp.concatenate([jnp.concatenate(part, axis=1) for part in lhs], axis=0)
                return dot(lhs, prob[t, i])

            def finish(n, side, qb):
                base = side * (HEAD + 16)
                out = n[base:base + HEAD] / n[base + HEAD:base + HEAD + 1]
                stage_a[i, qb] = out.astype(jnp.bfloat16)

                @pl.when(qb != me)
                def _():
                    back_copy(p, i, qb).start()

            def two(s):
                units = (5 - 2 * s, 4 - 2 * s)
                sums = [combine(t) for t in units]
                for t, n in zip(units, sums):
                    paired, low, high, _ = unit_of(t)
                    finish(n, 0, low)

                    @pl.when(paired)
                    def _():
                        finish(n, 1, high)

            each(3, two)
            ar[p, i, me] = stage_a[i, me]

        gather_values(0)
        gather_values(1)

        @pl.when(first)
        def _():
            wide_out_total().wait()

        def project_out(i):
            total(p, A + i).wait_recv()
            part = ar[p, i].reshape(512, ROWS).T
            for t in range(4):
                cols = pl.ds(t * 256, 256)
                before = xs[:, cols].astype(jnp.float32) if i == 0 else mixed[:, cols]
                mixed[:, cols] = before + dot(part, wa[3, pl.ds(i * 512, 512), cols])

        project_out(0)
        project_out(1)
        nb[...] = rms(mixed[...], gain_ref[1:2]).astype(jnp.bfloat16)

        @pl.when(first)
        def _():
            wide(0).wait()

        def expand(t):
            cols = pl.ds(pl.multiple_of(t * 2048, 2048), 2048)
            hidden[:, cols] = gelu(dot(nb[...], wu[:, cols])).astype(jnp.bfloat16)

        each(FF // 2048, expand)

        for kind in (K, Q, V, V + 1, A, A + 1):
            total(p, kind).wait_send()

        @pl.when(first)
        def _():
            wide(1).wait()

        def lower(t):
            @pl.when(t < 4)
            def _():
                cols = pl.ds(pl.multiple_of(t * 256, 256), 256)
                o_ref[:, cols] = (mixed[:, cols] + dot(hidden[...], wd[:, cols])).astype(
                    jnp.bfloat16
                )

            @pl.when(t < 4)
            def _():
                swap_out(t)

            @pl.when(t > 0)
            def _():
                compose(t - 1)

        @pl.when(first)
        def _():
            each(5, lower)

        @pl.when(p == 1)
        def _():
            o_ref[...] = (mixed[...] + dot(hidden[...], wd[...])).astype(jnp.bfloat16)

        @pl.when(first)
        def _():
            each(4, scan)
            each(4, hand_over)
            each(4, collect)

            @pl.when((h + y + core) == 0)
            def _():
                xs[...] = x_ref[...]

        return carry

    theirs = pl.ds(pl.multiple_of((1 - core) * 128, 128), 128)
    mine = pl.ds(pl.multiple_of(core * 128, 128), 128)
    is_low = core == 0

    def half(n):
        return pl.ds(pl.multiple_of(n * 256, 256), 256)

    def low_gain(n):
        return jnp.where(is_low, coarse_ref[:, half(n)], gains[8, :, half(n)])

    def high_gain(n):
        return jnp.where(is_low, gains[8, :, half(n)], coarse_ref[:, half(n)])

    def swap_copy(n):
        return remote(
            fine.at[n, theirs], half_in.at[n], csend_sem.at[0, n], crecv_sem.at[0, n], partner
        )

    def give_copy(n):
        return remote(
            given.at[n], corrected.at[n], csend_sem.at[1, n], crecv_sem.at[1, n], partner
        )

    def depth_copy(n, trip, i):
        step = depth_step(i)
        dev, dest = depth_peer(*step)
        if trip == 0:
            src = comp.at[n, pl.ds(pl.multiple_of(dest * 16, 16), 16)]
            dst = depth_a.at[n, chip]
        else:
            src, dst = depth_u.at[n, dest], depth_r.at[n, chip]
        return remote(src, dst, dsend_sem.at[n, trip], drecv_sem.at[n, trip], dev)

    def depth_total(n, trip):
        some = (depth_a, depth_r)[trip].at[n, pl.ds(0, 7)]
        return remote(some, some, dsend_sem.at[n, trip], drecv_sem.at[n, trip], partner)

    def swap_out(n):
        lead = jnp.where((h + y + core) == 0, 0.0, 1.0)
        a = o_ref[:, half(n)].astype(jnp.float32)
        b = (lead * coarse_ref[:, half(n)]) * x_ref[:, half(n)].astype(jnp.float32)
        fine[n] = (a - b).astype(jnp.bfloat16)
        swap_copy(n).start()

    def compose(n):
        @pl.when(n == 0)
        def _():
            gain_total().wait()

        swap_copy(n).wait()
        own, other = fine[n, mine, :].astype(jnp.float32), half_in[n].astype(jnp.float32)
        low, high = jnp.where(is_low, own, other), jnp.where(is_low, other, own)
        comp[n] = (high + high_gain(n) * low).astype(jnp.bfloat16)
        each(7, lambda i: depth_copy(n, 0, i).start())
        depth_a[n, chip] = comp[n, pl.ds(pl.multiple_of(chip * 16, 16), 16), :]

    def scan(n):
        depth_total(n, 0).wait_recv()
        u = jnp.zeros((16, 256), jnp.float32)
        for k in range(8):
            depth_u[n, k] = u.astype(jnp.bfloat16)
            u = depth_a[n, k].astype(jnp.float32) + gains[k, :, half(n)] * u
        each(7, lambda i: depth_copy(n, 1, i).start())
        depth_r[n, chip] = depth_u[n, chip]

    def hand_over(n):
        depth_total(n, 1).wait_recv()
        back = jnp.concatenate([depth_r[n, k] for k in range(8)], axis=0).astype(jnp.float32)
        own, other = fine[n, mine, :].astype(jnp.float32), half_in[n].astype(jnp.float32)
        after = jnp.where(is_low, own, other) + low_gain(n) * back
        given[n] = jnp.where(is_low, after, back).astype(jnp.bfloat16)
        give_copy(n).start()
        xs[mine, half(n)] = jnp.where(is_low, back, after).astype(jnp.bfloat16)

    def collect(n):
        depth_total(n, 0).wait_send()
        depth_total(n, 1).wait_send()
        give_copy(n).wait()
        xs[theirs, half(n)] = corrected[n]

    lax.fori_loop(0, 2, one_pass, 0)


def on_device(interfaces, doc_ids, w_attn, w_up, w_down, norm_gains, coarse_gain):
    x = interfaces.reshape(ROWS, D)
    doc = doc_ids.reshape(GROUPS, 1, ROWS)
    bf, f32 = jnp.bfloat16, jnp.float32
    vmem = pl.BlockSpec(memory_space=pltpu.VMEM)
    hbm = pl.BlockSpec(memory_space=pl.ANY)
    out = pl.pallas_call(
        kernel,
        out_shape=pltpu.VMEM((ROWS, D), bf),
        in_specs=[hbm] * 7,
        out_specs=vmem,
        scratch_shapes=[
            pltpu.VMEM((ROWS, D), bf),
            pltpu.VMEM((GROUPS, 1, ROWS), jnp.int32),
            pltpu.VMEM((2, D), f32),
            pltpu.VMEM((1, D), f32),
            pltpu.VMEM((4, D, D), bf),
            pltpu.VMEM((D, FF), bf),
            pltpu.VMEM((FF, D), bf),
            pltpu.VMEM((ROWS, D), bf),
            pltpu.VMEM((ROWS, D), bf),
            pltpu.VMEM((2, GROUPS, ROWS, LANES), bf),
            pltpu.VMEM((2, GROUPS, HEAD, ROWS), bf),
            pltpu.VMEM((2, GROUPS, ROWS, LANES), bf),
            pltpu.VMEM((2, GROUPS, ROWS, LANES), bf),
            pltpu.VMEM((2, 2, GROUPS, HEAD, ROWS), bf),
            pltpu.VMEM((GROUPS * SPAN, ROWS, ROWS), bf),
            pltpu.VMEM((6, 2, SPAN * ROWS, ROWS), bf),
            pltpu.VMEM((2, GROUPS, HEAD, ROWS), bf),
            pltpu.VMEM((2, 2, GROUPS, HEAD, ROWS), bf),
            pltpu.VMEM((ROWS, D), f32),
            pltpu.VMEM((ROWS, FF), bf),
            pltpu.VMEM((10, 1, D), f32),
            pltpu.VMEM((4, ROWS, 256), bf),
            pltpu.VMEM((4, 128, 256), bf),
            pltpu.VMEM((4, 128, 256), bf),
            pltpu.VMEM((4, 8, 16, 256), bf),
            pltpu.VMEM((4, 8, 16, 256), bf),
            pltpu.VMEM((4, 8, 16, 256), bf),
            pltpu.VMEM((4, 128, 256), bf),
            pltpu.VMEM((4, 128, 256), bf),
            pltpu.SemaphoreType.DMA((5,)),
            pltpu.SemaphoreType.DMA((3, 4)),
            pltpu.SemaphoreType.DMA((3,)),
            pltpu.SemaphoreType.DMA((6,)),
            pltpu.SemaphoreType.DMA((2, 6)),
            pltpu.SemaphoreType.DMA((2, 8)),
            pltpu.SemaphoreType.DMA((2,)),
            pltpu.SemaphoreType.DMA((4, 2)),
            pltpu.SemaphoreType.DMA((4, 2)),
            pltpu.SemaphoreType.DMA((3, 4)),
            pltpu.SemaphoreType.DMA((3, 4)),
        ],
        compiler_params=pltpu.CompilerParams(
            collective_id=0, has_side_effects=True, vmem_limit_bytes=60 * 2**20
        ),
        name="cycle",
    )(
        x,
        doc,
        norm_gains.reshape(2, D),
        coarse_gain.reshape(1, D),
        w_attn.reshape(4, D, D),
        w_up.reshape(D, FF),
        w_down.reshape(FF, D),
    )
    return out.reshape(1, 1, ROWS, D)


def solution(mesh):
    split = Mesh(
        mesh.devices.reshape(2, 4, 2, 4, 2), ("depth_0", "depth_1", "depth_2", "seq_0", "seq_1")
    )
    in_specs = (
        P(DEPTH, None, SEQ, None),
        P(),
        P(DEPTH, None, None, None, None),
        P(DEPTH, None, None, None),
        P(DEPTH, None, None, None),
        P(DEPTH, None, None, None),
        P(DEPTH, None),
    )
    out_specs = P(DEPTH, None, SEQ, None)
    return jax.shard_map(
        on_device, mesh=split, in_specs=in_specs, out_specs=out_specs, check_vma=False
    )
```

```python
import functools

import jax
import jax.numpy as jnp
from jax import lax
from jax.experimental import pallas as pl
from jax.experimental.pallas import tpu as pltpu
from jax.sharding import Mesh
from jax.sharding import PartitionSpec as P

D = 1024
FF = 4096
ROWS = 256
LANES = 128
HEAD = 64
GROUPS = 8
SPAN = 5
SEQ = ("seq_0", "seq_1")
DEPTH = ("depth_0", "depth_1", "depth_2")
MESH = pl.DeviceIdType.MESH
K, Q, V, A = 0, 1, 2, 4
NT = (((1,), (1,)), ((), ()))


def dot(a, b):
    return jnp.dot(a, b, preferred_element_type=jnp.float32)


def each(count, action):
    def body(i, carry):
        action(i)
        return carry

    lax.fori_loop(0, count, body, 0)


def row_step(u):
    return (2 - u) + lax.div(u, 2) * (7 - 2 * u)


def seq_step(i):
    u = lax.div(i, 2)
    return row_step(u), 1 - (i - 2 * u)


def depth_step(i):
    u = lax.div(i, 4)
    return 1 - u, row_step(i - 4 * u)


def gelu(x):
    inner = x * (x * x * (0.044715 * 0.7978845608028654) + 0.7978845608028654)
    part = 0.5 * x
    return part * jnp.tanh(inner) + part


def rms(value, gain):
    return value * lax.rsqrt(jnp.mean(value * value, axis=-1, keepdims=True) + 1e-05) * gain


def kernel(
    x_hbm, doc_hbm, gain_hbm, coarse_hbm, wa_hbm, wu_hbm, wd_hbm, o_ref,
    x_ref, doc_ref, gain_ref, coarse_ref, wa, wu, wd, xs, nb, stage, stage_v, kr, qr, vr, mask, prob, stage_a, ar, mixed, hidden,
    gains, fine, half_in, comp, depth_a, depth_u, depth_r, given, corrected,
    in_sem, w_sem, wide_sem, send_sem, recv_sem, q_sem, g_sem, dsend_sem, drecv_sem, csend_sem, crecv_sem,
):
    h, y, core = (lax.axis_index(a) for a in DEPTH)
    z, c = (lax.axis_index(a) for a in SEQ)
    me = 2 * z + c
    chip = 4 * h + y
    partner = (h, y, 1 - core, z, c)

    def seq_peer(dz, dx):
        pz, pc = lax.rem(z + 4 + dz, 4), lax.rem(c + dx, 2)
        return (h, y, core, pz, pc), 2 * pz + pc

    def depth_peer(dh, dy):
        ph, py = lax.rem(h + dh, 2), lax.rem(y + 4 + dy, 4)
        return (ph, py, core, z, c), 4 * ph + py

    def remote(src, dst, ss, rs, dev):
        return pltpu.make_async_remote_copy(
            src_ref=src, dst_ref=dst, send_sem=ss, recv_sem=rs, device_id=dev, device_id_type=MESH
        )

    def tile_cols(n):
        return pl.ds(pl.multiple_of(lax.rem(z + row_step(n), 4) * 256, 256), 256)

    def narrow(which, n):
        cols = tile_cols(n)
        return pltpu.make_async_copy(
            wa_hbm.at[which, :, cols], wa.at[which, :, cols], w_sem.at[which, n]
        )

    def wide(i):
        src, dst = ((wu_hbm, wu), (wd_hbm, wd))[i]
        return pltpu.make_async_copy(src, dst, wide_sem.at[i])

    def wide_out(j):
        i = lax.rem(j, 2)
        rows = pl.ds(pl.multiple_of(j * HEAD, HEAD), HEAD)
        place = pl.ds(pl.multiple_of(i * 512 + lax.div(j, 2) * HEAD, HEAD), HEAD)
        return pltpu.make_async_copy(wa_hbm.at[3, rows], wa.at[3, place], wide_sem.at[2])

    def wide_out_total():
        return pltpu.make_async_copy(wa_hbm.at[3], wa.at[3], wide_sem.at[2])

    def entry(i):
        src = (x_hbm, gain_hbm, x_hbm, doc_hbm, coarse_hbm)[i]
        dst = (xs, gain_ref, x_ref, doc_ref, coarse_ref)[i]
        return pltpu.make_async_copy(src, dst, in_sem.at[i])

    entry(0).start()
    entry(1).start()
    each(4, lambda n: narrow(1, n).start())

    barrier = pltpu.get_barrier_semaphore()

    def greet(dev):
        pl.semaphore_signal(barrier, inc=1, device_id=dev, device_id_type=MESH)

    each(7, lambda i: greet(seq_peer(*seq_step(i))[0]))
    each(7, lambda i: greet(depth_peer(*depth_step(i))[0]))
    greet(partner)
    entry(0).wait()
    entry(1).wait()
    each(4, lambda n: narrow(0, n).start())
    each(4, lambda n: narrow(2, n).start())
    for i in range(2, 5):
        entry(i).start()

    gain_swap = remote(coarse_ref, gains.at[8], csend_sem.at[2, 0], crecv_sem.at[2, 0], partner)

    def gain_copy(i):
        dev, _ = depth_peer(*depth_step(i))
        return remote(gains.at[9], gains.at[chip], g_sem.at[0], g_sem.at[1], dev)

    def gain_total():
        some = gains.at[pl.ds(0, 7)]
        return remote(some, some, g_sem.at[0], g_sem.at[1], partner)

    def seq_copy(p, kind, i):
        dev, dest = seq_peer(*seq_step(i))
        if kind == K:
            src, dst = stage.at[0, dest], kr.at[p, me]
        elif kind == Q:
            src, dst = stage.at[1, dest], qr.at[p, me]
        else:
            src, dst = stage_v.at[kind - V, dest], vr.at[p, kind - V, me]
        got = q_sem.at[p, me] if kind == Q else recv_sem.at[p, kind]
        return remote(src, dst, send_sem.at[kind], got, dev)

    def query_arrival(p, who):
        dst = qr.at[p, who]
        return remote(dst, dst, send_sem.at[Q], q_sem.at[p, who], partner)

    def back_copy(p, i, dest):
        pz = lax.div(dest, 2)
        dev = (h, y, core, pz, dest - 2 * pz)
        return remote(
            stage_a.at[i, dest], ar.at[p, i, me], send_sem.at[A + i], recv_sem.at[p, A + i], dev
        )

    def total(p, kind):
        seven = pl.ds(0, 7)
        if kind == K:
            some = kr.at[p, seven]
        elif kind == Q:
            some = qr.at[p, seven]
        elif kind < A:
            some = vr.at[p, kind - V, seven]
        else:
            some = ar.at[p, kind - A, seven]
        return remote(some, some, send_sem.at[kind], recv_sem.at[p, kind], partner)

    lane = lax.broadcasted_iota(jnp.int32, (ROWS, LANES), 1)

    def one_pass(p, carry):
        first = p == 0
        nb[...] = rms(xs[...].astype(jnp.float32), gain_ref[0:1]).astype(jnp.bfloat16)

        def project(which, kind, store):
            def tile(u):
                @pl.when(first)
                def _():
                    narrow(which, u).wait()

                base = 2 * lax.rem(z + row_step(u), 4)
                store(base, dot(nb[...], wa[which, :, tile_cols(u)]).astype(jnp.bfloat16))
                if kind == K:

                    @pl.when(first & (u == 0))
                    def _():
                        pl.semaphore_wait(barrier, 15)

                if kind != V:
                    seq_copy(p, kind, 2 * u).start()

                    @pl.when(u < 3)
                    def _():
                        seq_copy(p, kind, 2 * u + 1).start()

            each(4, tile)

        def store_k(base, r):
            stage[0, base] = r[:, :LANES]
            stage[0, base + 1] = r[:, LANES:]

        def store_q(base, r):
            r = r * jnp.bfloat16(0.125)
            stage[1, base] = r[:, :LANES]
            stage[1, base + 1] = r[:, LANES:]

        def store_v(base, r):
            r = r.T
            for j in range(2):
                for i in range(2):
                    stage_v[i, base + j] = r[j * LANES + i * HEAD:j * LANES + (i + 1) * HEAD]

        project(1, K, store_k)
        kr[p, me] = stage[0, me]
        project(0, Q, store_q)
        qr[p, me] = stage[1, me]
        project(2, V, store_v)
        each(7, lambda i: seq_copy(p, V, i).start())
        each(7, lambda i: seq_copy(p, V + 1, i).start())
        for i in range(2):
            vr[p, i, me] = stage_v[i, me]

        @pl.when(first)
        def _():
            each(16, lambda j: wide_out(j).start())
            wide(0).start()
            wide(1).start()
            for i in range(2, 5):
                entry(i).wait()
            gain_swap.start()
            gain_swap.wait()
            gains[9] = coarse_ref[...] * gains[8]
            gains[chip] = gains[9]
            each(7, lambda i: gain_copy(i).start())

            def build(qb, carry):
                doc_q = doc_ref[qb].astype(jnp.float32)

                def inner(d, carry):
                    doc_k = doc_ref[qb - d].astype(jnp.float32)
                    doc_k = jnp.broadcast_to(doc_k, (LANES, ROWS)).T
                    doc_k = jnp.concatenate([doc_k, doc_k], axis=1)
                    kpos = lax.broadcasted_iota(jnp.int32, (ROWS, ROWS), 0) - d * ROWS
                    qpos = lax.broadcasted_iota(jnp.int32, (ROWS, ROWS), 1)
                    ok = (kpos <= qpos) & (doc_k == doc_q)
                    mask[qb * SPAN + d] = jnp.where(ok, jnp.inf, 0.0).astype(jnp.bfloat16)
                    return carry

                return lax.fori_loop(0, jnp.minimum(qb, SPAN - 1) + 1, inner, carry)

            lax.fori_loop(0, GROUPS, build, 0)

        total(p, K).wait_recv()
        own = jnp.where(me >= 4, me - 4, jnp.where((me == 0) | (me == 3), 4, 5))

        def unit_of(t):
            g = lax.div(t, 2)
            near = jnp.where((z == 1) | (z == 2), 0, 2)
            full = jnp.where(lax.rem(g + z, 2) == lax.rem(z, 2), near, 2 - near)
            late = jnp.where(g == 1, near, 2 - near)
            base = jnp.where(
                z < 2,
                jnp.where(g == 0, 4, late),
                jnp.where(g == 2, 4, full),
            )
            unit = base + lax.rem(own + t, 2)
            paired = unit >= 4
            low = jnp.where(paired, unit - 4, unit + 4)
            high = jnp.where(paired, 3 - low, low)
            split = jnp.where(paired, low + 1, SPAN)
            return paired, low, high, split

        def weigh(t):
            paired, low, high, split = unit_of(t)

            @pl.when(low != me)
            def _():
                query_arrival(p, low).wait_recv()

            @pl.when(paired & (high != me))
            def _():
                query_arrival(p, high).wait_recv()

            for j in range(SPAN):
                is_low = j < split
                qb = jnp.where(is_low, low, high)
                d = jnp.where(is_low, j, j - split)
                q = qr[p, qb]
                zero = jnp.zeros_like(q)
                parts = jnp.where(lane < HEAD, q, zero), jnp.where(lane < HEAD, zero, q)
                keys = kr[p, qb - d]
                m = mask[qb * SPAN + d]
                for i in range(2):
                    s = lax.dot_general(keys, parts[i], NT, preferred_element_type=jnp.float32)
                    e = jnp.exp(s).astype(jnp.bfloat16)
                    prob[t, i, pl.ds(j * ROWS, ROWS)] = jnp.minimum(e, m)

        each(6, weigh)

        def gather_values(i):
            total(p, V + i).wait_recv()

            def combine(t):
                _, low, high, split = unit_of(t)
                lhs = [[], [], [], []]
                for j in range(SPAN):
                    is_low = j < split
                    block = jnp.where(is_low, low - j, high - j + split)
                    v = vr[p, i, block]
                    ones = jnp.ones((16, ROWS), jnp.bfloat16)
                    lhs[0].append(jnp.where(is_low, v, 0))
                    lhs[1].append(jnp.where(is_low, ones, 0))
                    lhs[2].append(jnp.where(is_low, 0, v))
                    lhs[3].append(jnp.where(is_low, 0, ones))
                lhs = jnp.concatenate([jnp.concatenate(part, axis=1) for part in lhs], axis=0)
                return dot(lhs, prob[t, i])

            def finish(n, side, qb):
                base = side * (HEAD + 16)
                out = n[base:base + HEAD] / n[base + HEAD:base + HEAD + 1]
                stage_a[i, qb] = out.astype(jnp.bfloat16)

                @pl.when(qb != me)
                def _():
                    back_copy(p, i, qb).start()

            def two(s):
                units = (5 - 2 * s, 4 - 2 * s)
                sums = [combine(t) for t in units]
                for t, n in zip(units, sums):
                    paired, low, high, _ = unit_of(t)
                    finish(n, 0, low)

                    @pl.when(paired)
                    def _():
                        finish(n, 1, high)

            each(3, two)
            ar[p, i, me] = stage_a[i, me]

        gather_values(0)
        gather_values(1)

        @pl.when(first)
        def _():
            wide_out_total().wait()

        def project_out(i):
            total(p, A + i).wait_recv()
            part = ar[p, i].reshape(512, ROWS).T
            for t in range(4):
                cols = pl.ds(t * 256, 256)
                before = xs[:, cols].astype(jnp.float32) if i == 0 else mixed[:, cols]
                mixed[:, cols] = before + dot(part, wa[3, pl.ds(i * 512, 512), cols])

        project_out(0)
        project_out(1)
        nb[...] = rms(mixed[...], gain_ref[1:2]).astype(jnp.bfloat16)

        @pl.when(first)
        def _():
            wide(0).wait()

        hidden[...] = gelu(dot(nb[...], wu[...])).astype(jnp.bfloat16)

        for kind in (K, Q, V, V + 1, A, A + 1):
            total(p, kind).wait_send()

        @pl.when(first)
        def _():
            wide(1).wait()

        def lower(t):
            @pl.when(t < 4)
            def _():
                cols = pl.ds(pl.multiple_of(t * 256, 256), 256)
                o_ref[:, cols] = (mixed[:, cols] + dot(hidden[...], wd[:, cols])).astype(
                    jnp.bfloat16
                )

            @pl.when(t < 4)
            def _():
                swap_out(t)

            @pl.when(t > 0)
            def _():
                compose(t - 1)

        @pl.when(first)
        def _():
            each(5, lower)

        @pl.when(p == 1)
        def _():
            o_ref[...] = (mixed[...] + dot(hidden[...], wd[...])).astype(jnp.bfloat16)

        @pl.when(first)
        def _():
            each(4, scan)
            each(4, hand_over)
            each(4, collect)

            @pl.when((h + y + core) == 0)
            def _():
                xs[...] = x_ref[...]

        return carry

    theirs = pl.ds(pl.multiple_of((1 - core) * 128, 128), 128)
    mine = pl.ds(pl.multiple_of(core * 128, 128), 128)
    is_low = core == 0

    def half(n):
        return pl.ds(pl.multiple_of(n * 256, 256), 256)

    def low_gain(n):
        return jnp.where(is_low, coarse_ref[:, half(n)], gains[8, :, half(n)])

    def high_gain(n):
        return jnp.where(is_low, gains[8, :, half(n)], coarse_ref[:, half(n)])

    def swap_copy(n):
        return remote(
            fine.at[n, theirs], half_in.at[n], csend_sem.at[0, n], crecv_sem.at[0, n], partner
        )

    def give_copy(n):
        return remote(
            given.at[n], corrected.at[n], csend_sem.at[1, n], crecv_sem.at[1, n], partner
        )

    def depth_copy(n, trip, i):
        step = depth_step(i)
        dev, dest = depth_peer(*step)
        if trip == 0:
            src = comp.at[n, pl.ds(pl.multiple_of(dest * 16, 16), 16)]
            dst = depth_a.at[n, chip]
        else:
            src, dst = depth_u.at[n, dest], depth_r.at[n, chip]
        return remote(src, dst, dsend_sem.at[n, trip], drecv_sem.at[n, trip], dev)

    def depth_total(n, trip):
        some = (depth_a, depth_r)[trip].at[n, pl.ds(0, 7)]
        return remote(some, some, dsend_sem.at[n, trip], drecv_sem.at[n, trip], partner)

    def swap_out(n):
        lead = jnp.where((h + y + core) == 0, 0.0, 1.0)
        a = o_ref[:, half(n)].astype(jnp.float32)
        b = (lead * coarse_ref[:, half(n)]) * x_ref[:, half(n)].astype(jnp.float32)
        fine[n] = (a - b).astype(jnp.bfloat16)
        swap_copy(n).start()

    def compose(n):
        @pl.when(n == 0)
        def _():
            gain_total().wait()

        swap_copy(n).wait()
        own, other = fine[n, mine, :].astype(jnp.float32), half_in[n].astype(jnp.float32)
        low, high = jnp.where(is_low, own, other), jnp.where(is_low, other, own)
        comp[n] = (high + high_gain(n) * low).astype(jnp.bfloat16)
        each(7, lambda i: depth_copy(n, 0, i).start())
        depth_a[n, chip] = comp[n, pl.ds(pl.multiple_of(chip * 16, 16), 16), :]

    def scan(n):
        depth_total(n, 0).wait_recv()
        u = jnp.zeros((16, 256), jnp.float32)
        for k in range(8):
            depth_u[n, k] = u.astype(jnp.bfloat16)
            u = depth_a[n, k].astype(jnp.float32) + gains[k, :, half(n)] * u
        each(7, lambda i: depth_copy(n, 1, i).start())
        depth_r[n, chip] = depth_u[n, chip]

    def hand_over(n):
        depth_total(n, 1).wait_recv()
        back = jnp.concatenate([depth_r[n, k] for k in range(8)], axis=0).astype(jnp.float32)
        own, other = fine[n, mine, :].astype(jnp.float32), half_in[n].astype(jnp.float32)
        after = jnp.where(is_low, own, other) + low_gain(n) * back
        given[n] = jnp.where(is_low, after, back).astype(jnp.bfloat16)
        give_copy(n).start()
        xs[mine, half(n)] = jnp.where(is_low, back, after).astype(jnp.bfloat16)

    def collect(n):
        depth_total(n, 0).wait_send()
        depth_total(n, 1).wait_send()
        give_copy(n).wait()
        xs[theirs, half(n)] = corrected[n]

    lax.fori_loop(0, 2, one_pass, 0)


def on_device(interfaces, doc_ids, w_attn, w_up, w_down, norm_gains, coarse_gain):
    x = interfaces.reshape(ROWS, D)
    doc = doc_ids.reshape(GROUPS, 1, ROWS)
    bf, f32 = jnp.bfloat16, jnp.float32
    vmem = pl.BlockSpec(memory_space=pltpu.VMEM)
    hbm = pl.BlockSpec(memory_space=pl.ANY)
    out = pl.pallas_call(
        kernel,
        out_shape=pltpu.VMEM((ROWS, D), bf),
        in_specs=[hbm] * 7,
        out_specs=vmem,
        scratch_shapes=[
            pltpu.VMEM((ROWS, D), bf),
            pltpu.VMEM((GROUPS, 1, ROWS), jnp.int32),
            pltpu.VMEM((2, D), f32),
            pltpu.VMEM((1, D), f32),
            pltpu.VMEM((4, D, D), bf),
            pltpu.VMEM((D, FF), bf),
            pltpu.VMEM((FF, D), bf),
            pltpu.VMEM((ROWS, D), bf),
            pltpu.VMEM((ROWS, D), bf),
            pltpu.VMEM((2, GROUPS, ROWS, LANES), bf),
            pltpu.VMEM((2, GROUPS, HEAD, ROWS), bf),
            pltpu.VMEM((2, GROUPS, ROWS, LANES), bf),
            pltpu.VMEM((2, GROUPS, ROWS, LANES), bf),
            pltpu.VMEM((2, 2, GROUPS, HEAD, ROWS), bf),
            pltpu.VMEM((GROUPS * SPAN, ROWS, ROWS), bf),
            pltpu.VMEM((6, 2, SPAN * ROWS, ROWS), bf),
            pltpu.VMEM((2, GROUPS, HEAD, ROWS), bf),
            pltpu.VMEM((2, 2, GROUPS, HEAD, ROWS), bf),
            pltpu.VMEM((ROWS, D), f32),
            pltpu.VMEM((ROWS, FF), bf),
            pltpu.VMEM((10, 1, D), f32),
            pltpu.VMEM((4, ROWS, 256), bf),
            pltpu.VMEM((4, 128, 256), bf),
            pltpu.VMEM((4, 128, 256), bf),
            pltpu.VMEM((4, 8, 16, 256), bf),
            pltpu.VMEM((4, 8, 16, 256), bf),
            pltpu.VMEM((4, 8, 16, 256), bf),
            pltpu.VMEM((4, 128, 256), bf),
            pltpu.VMEM((4, 128, 256), bf),
            pltpu.SemaphoreType.DMA((5,)),
            pltpu.SemaphoreType.DMA((3, 4)),
            pltpu.SemaphoreType.DMA((3,)),
            pltpu.SemaphoreType.DMA((6,)),
            pltpu.SemaphoreType.DMA((2, 6)),
            pltpu.SemaphoreType.DMA((2, 8)),
            pltpu.SemaphoreType.DMA((2,)),
            pltpu.SemaphoreType.DMA((4, 2)),
            pltpu.SemaphoreType.DMA((4, 2)),
            pltpu.SemaphoreType.DMA((3, 4)),
            pltpu.SemaphoreType.DMA((3, 4)),
        ],
        compiler_params=pltpu.CompilerParams(
            collective_id=0, has_side_effects=True, vmem_limit_bytes=60 * 2**20
        ),
        name="cycle",
    )(
        x,
        doc,
        norm_gains.reshape(2, D),
        coarse_gain.reshape(1, D),
        w_attn.reshape(4, D, D),
        w_up.reshape(D, FF),
        w_down.reshape(FF, D),
    )
    return out.reshape(1, 1, ROWS, D)


def solution(mesh):
    split = Mesh(
        mesh.devices.reshape(2, 4, 2, 4, 2), ("depth_0", "depth_1", "depth_2", "seq_0", "seq_1")
    )
    in_specs = (
        P(DEPTH, None, SEQ, None),
        P(),
        P(DEPTH, None, None, None, None),
        P(DEPTH, None, None, None),
        P(DEPTH, None, None, None),
        P(DEPTH, None, None, None),
        P(DEPTH, None),
    )
    out_specs = P(DEPTH, None, SEQ, None)
    return jax.shard_map(
        on_device, mesh=split, in_specs=in_specs, out_specs=out_specs, check_vma=False
    )
```
